512 devices in a mesh: ax: 32 (over x_lo, z), az: 16 (over y, x_hi, core).
Axes of the slice: x: 4 (x_hi: 2, x_lo: 2; x = x_hi * 2 + x_lo), y: 4, z: 16, core: 2. Of those that a mesh axis runs over, the one named last changes fastest.
Arguments:
- conserved: float32 [5, 256, 1024, 128], P(None, 'ax', 'az'), may hold values from -0.6 to 3, as said below
- panel_cells: int32 [262144], P(('ax', 'az')), may hold values from 0 to 65535
- panel_counts: int32 [512], P(('ax', 'az')), may hold values from 1 to 512, 131072 in all
- time_bins: int32 [262144, 64], P(('ax', 'az')), may hold values from 0 to 1023
- amplitudes: float32 [262144, 64], P(('ax', 'az')), may hold values from 0.5 to 2
Outputs:
- section: float32 [5, 256, 1024, 128], P(None, 'ax', 'az')
- signal: float32 [64, 1024], P(None, ('ax', 'az'))
The draws below stay inside these ranges and needn't reach their ends.
Inputs may be any that keep to these rules, and one draw needn't show every extreme that they name: `conserved`: component 0 lies in 0.7 to 1.3, components 1 to 3 in -0.6 to 0.6, component 4 in 2.0 to 3.0. `panel_counts`: some device has exactly 512 live panel slots, each device at least one.
All inputs are finite; a program needn't handle non-finite values.
Results may differ from the reference program's by a relative error of at most 0.000076.
Values sent between devices are 32-bit elements; how exact they have to be, the bound alone decides.
A program may use at most 64 MiB of HBM per device.

```python
import math
import jax
import jax.numpy as jnp
import numpy as np
from jax import lax

PLANES_DEV = 8
RADIAL = 128
AZIMUTH = 1024
CYCLES = 8
OBSERVERS = 64
BINS = 1024
PAN_DEV = 512
PLANES = 256
CELLS_DEV = 65536
PANELS = 262144
N_AZ = 16
DEVICES = 512


def draw_conserved(key, part):
    shape = (PLANES, AZIMUTH, RADIAL)
    key_density = jax.random.fold_in(key, 11)
    key_moment = jax.random.fold_in(key, 12)
    key_energy = jax.random.fold_in(key, 13)
    fluid_rho_value = jax.random.uniform(key_density, shape, jnp.float32, 0.8, 1.2)
    moment = jax.random.uniform(key_moment, (3,) + shape, jnp.float32, -0.6, 0.6)
    overall_heat_work = jax.random.uniform(key_energy, shape, jnp.float32, 2.2, 2.8)
    return jnp.concatenate([fluid_rho_value[None], moment, overall_heat_work[None]], axis=0)


def plant(array, key, low, largest):
    index_at = [jax.random.randint(jax.random.fold_in(key, axis), (), 0, length) for axis, length in enumerate(array.shape)]
    main_axis = array.shape.index(max(array.shape))
    beside = index_at[:main_axis] + [(index_at[main_axis] + 1) % array.shape[main_axis]] + index_at[main_axis + 1:]
    return array.at[tuple(index_at)].set(low).at[tuple(beside)].set(largest)


def shard_levels(rng, shape, pieces, smallest, high):
    def one(dim, blocks):
        heights = jax.random.uniform(jax.random.fold_in(jax.random.fold_in(rng, 6), dim), (blocks,), jnp.float32, smallest / len(pieces), high / len(pieces))
        return jnp.repeat(jnp.exp(heights), shape[dim] // blocks).reshape((-1,) + (1,) * (len(shape) - dim - 1))

    gain = one(*pieces[0])
    for cut in pieces[1:]:
        gain = gain * one(*cut)
    return gain


def profile(count, total, limit, skew):
    weights = [(1 << 20) // math.isqrt(standing ** skew) + 1 for standing in range(2, count + 1)]
    rest, holding = total - limit - (count - 1), [1] * (count - 1)
    while rest > 0:
        movable = [i for i in range(count - 1) if holding[i] < limit]
        whole, left = sum([weights[i] for i in movable]), rest
        for i in movable:
            addition = min(limit - holding[i], max(1, left * weights[i] // whole), rest)
            holding[i] = holding[i] + addition
            rest = rest - addition
    return np.array([limit] + holding)


def ragged(stream_key, count, total, limit, lean):
    if count == 2:
        one = jax.random.randint(stream_key, (), max(1, total - limit), min(limit, total - 1) + 1)
        return jnp.stack([one, total - one])
    lengths = jnp.asarray(profile(count, total, limit, lean), jnp.int32)
    pairs = (count - 1) // 2
    donor, sink = lengths[1:1 + 2 * pairs:2], lengths[2:2 + 2 * pairs:2]
    slack = jnp.minimum(donor - 1, limit - sink)
    moved = jax.random.randint(jax.random.fold_in(stream_key, 1), (pairs,), 0, 1 << 20) % (slack + 1)
    lengths = lengths.at[1:1 + 2 * pairs:2].set(donor - moved).at[2:2 + 2 * pairs:2].set(sink + moved)
    return lengths[jax.random.permutation(jax.random.fold_in(stream_key, 2), count)]


def setup_inputs(seed: int = 0) -> dict:
    splits = jax.random.split(jax.random.key(seed), 6)
    return {
        "conserved": draw_conserved(jax.random.fold_in(splits[5], 71), 0),
        "panel_cells": plant(jax.random.randint(splits[1], (PANELS,), 0, CELLS_DEV), jax.random.fold_in(splits[1], 1), 0, CELLS_DEV - 1).astype(jnp.int32),
        "panel_counts": ragged(splits[2], DEVICES, PANELS // 2, PAN_DEV, 2).astype(jnp.int32),
        "time_bins": plant(jax.random.randint(splits[3], (PANELS, OBSERVERS), 0, BINS), jax.random.fold_in(splits[3], 1), 0, BINS - 1).astype(jnp.int32),
        "amplitudes": jnp.clip(jnp.exp(math.log(2.0) - 1.3862944 * jax.random.uniform(splits[4], (PANELS, OBSERVERS), jnp.float32) ** shard_levels(splits[4], (PANELS, OBSERVERS), ((0, 512),), -0.2, 0.2)), 0.5, 2.0),
    }


gas_factor = 0.4
time_step = 0.02
ref_pressure = 0.95


def primitives(conserved):
    fluid_rho_value = conserved[0]
    axial_vel = conserved[1] / fluid_rho_value
    radial_vel = conserved[2] / fluid_rho_value
    swirl_vel = conserved[3] / fluid_rho_value
    kinetic = 0.5 * (conserved[1] * axial_vel + conserved[2] * radial_vel + conserved[3] * swirl_vel)
    thermo_stress_level = gas_factor * (conserved[4] - kinetic)
    return jnp.stack([fluid_rho_value, axial_vel, radial_vel, swirl_vel, thermo_stress_level])


def flux_along(primitive, stream_heading):
    fluid_rho_value = primitive[0]
    thermo_stress_level = primitive[4]
    stream_speed = [primitive[1], primitive[2], primitive[3]]
    overall_heat_work = thermo_stress_level / gas_factor + 0.5 * fluid_rho_value * (stream_speed[0] * stream_speed[0] + stream_speed[1] * stream_speed[1] + stream_speed[2] * stream_speed[2])
    holder_buffer = stream_speed[stream_heading]
    divided_pieces = [fluid_rho_value * holder_buffer]
    for entry_number in range(3):
        forcing_contribution = fluid_rho_value * stream_speed[entry_number] * holder_buffer
        if entry_number == stream_heading:
            forcing_contribution = forcing_contribution + thermo_stress_level
        divided_pieces.append(forcing_contribution)
    divided_pieces.append((overall_heat_work + thermo_stress_level) * holder_buffer)
    return jnp.stack(divided_pieces)


def fourth_diff(padded, along_axis, length):
    near_diff = lax.slice_in_dim(padded, 3, length + 3, axis=along_axis) - lax.slice_in_dim(padded, 1, length + 1, axis=along_axis)
    far_diff = lax.slice_in_dim(padded, 4, length + 4, axis=along_axis) - lax.slice_in_dim(padded, 0, length, axis=along_axis)
    return (8.0 * near_diff - far_diff) / 12.0


def cycle_weights(length):
    modes = jnp.arange(length // 2 + 1).astype(jnp.float32)
    cutoff = 4.0 * (jnp.arange(CYCLES).astype(jnp.float32) + 1.0)
    return jnp.exp(-((modes[None, :] / cutoff[:, None]) ** 8))


def reference(conserved, panel_cells, panel_counts, time_bins, amplitudes):
    primitive = primitives(conserved)
    planes_all = conserved.shape[1]
    radial_all = conserved.shape[3]
    radius = jnp.arange(radial_all).astype(jnp.float32) + 0.5
    dtheta = 2.0 * math.pi / AZIMUTH
    axial_flux = flux_along(primitive, 0)
    radial_flux = flux_along(primitive, 1)
    swirl_flux = flux_along(primitive, 2)
    padded_x = jnp.pad(axial_flux, ((0, 0), (2, 2), (0, 0), (0, 0)))
    padded_t = jnp.pad(swirl_flux, ((0, 0), (0, 0), (2, 2), (0, 0)), mode="wrap")
    padded_r = jnp.pad(radial_flux * radius, ((0, 0), (0, 0), (0, 0), (2, 2)))
    tendency = -fourth_diff(padded_x, 1, planes_all)
    tendency = tendency - fourth_diff(padded_r, 3, radial_all) / radius
    tendency = tendency - fourth_diff(padded_t, 2, AZIMUTH) / (radius * dtheta)
    fluid_rho_value = primitive[0]
    radial_vel = primitive[2]
    swirl_vel = primitive[3]
    thermo_stress_level = primitive[4]
    zeros_field = jnp.zeros_like(fluid_rho_value)
    source = jnp.stack([zeros_field, zeros_field, (thermo_stress_level + fluid_rho_value * swirl_vel * swirl_vel) / radius, -fluid_rho_value * radial_vel * swirl_vel / radius, zeros_field])
    raw_section = conserved + time_step * (tendency + source)
    inner = raw_section[..., :CYCLES]
    spectrum = jnp.fft.rfft(inner, axis=2) * jnp.transpose(cycle_weights(AZIMUTH))[None, None, :, :]
    smooth = jnp.fft.irfft(spectrum, n=AZIMUTH, axis=2).astype(raw_section.dtype)
    section = jnp.concatenate([smooth, raw_section[..., CYCLES:]], axis=3)
    sector = AZIMUTH // N_AZ
    slots = jnp.arange(PANELS).astype(jnp.int32)
    device = slots // PAN_DEV
    ax_index = device // N_AZ
    az_index = device % N_AZ
    plane_local = panel_cells // (sector * radial_all)
    theta_local = (panel_cells // radial_all) % sector
    radial_index = panel_cells % radial_all
    flat = ((ax_index * PLANES_DEV + plane_local) * AZIMUTH + az_index * sector + theta_local) * radial_all + radial_index
    flat = flat.astype(jnp.int32)
    live = (slots % PAN_DEV) < panel_counts[device]
    sampled = jnp.where(live, thermo_stress_level.reshape(-1)[flat] - ref_pressure, 0.0)
    contrib = sampled[:, None] * amplitudes
    segment = (jnp.arange(OBSERVERS).astype(jnp.int32)[None, :] * BINS + time_bins).astype(jnp.int32)
    signal = jax.ops.segment_sum(contrib.reshape(-1), segment.reshape(-1), num_segments=OBSERVERS * BINS)
    return section, signal.reshape(OBSERVERS, BINS)
```

```python
import math

import jax
import jax.numpy as jnp
import numpy as np
from jax import lax
from jax.experimental import pallas as pl
from jax.experimental.pallas import tpu as pltpu
from jax.sharding import PartitionSpec as P

AZIMUTH = 1024
CYCLES = 8
OBSERVERS = 64
BINS = 1024
MESH = pl.DeviceIdType.MESH

gas_factor = 0.4
time_step = 0.02
ref_pressure = 0.95


def padded_2(value, sides, width, wrap):
    for axis, dim in sides:
        size, length = (lax.axis_size(axis), value.shape[dim])
        up = [(i, (i + 1) % size) for i in range(size if wrap else size - 1)]
        down = [(j, i) for i, j in up]
        last = lax.slice_in_dim(value, length - width, length, axis=dim)
        leading = lax.slice_in_dim(value, 0, width, axis=dim)
        before = lax.ppermute(last, axis, up)
        after = lax.ppermute(leading, axis, down)
        value = jnp.concatenate([before, value, after], axis=dim)
    return value


def primitives(conserved):
    fluid_rho_value = conserved[0]
    axial_vel = conserved[1] / fluid_rho_value
    radial_vel = conserved[2] / fluid_rho_value
    swirl_vel = conserved[3] / fluid_rho_value
    kinetic = 0.5 * (
        conserved[1] * axial_vel + conserved[2] * radial_vel + conserved[3] * swirl_vel
    )
    thermo_stress_level = gas_factor * (conserved[4] - kinetic)
    return jnp.stack([fluid_rho_value, axial_vel, radial_vel, swirl_vel, thermo_stress_level])


def flux_along(primitive, stream_heading):
    fluid_rho_value = primitive[0]
    thermo_stress_level = primitive[4]
    stream_speed = [primitive[1], primitive[2], primitive[3]]
    overall_heat_work = thermo_stress_level / gas_factor + 0.5 * fluid_rho_value * (
        stream_speed[0] * stream_speed[0]
        + stream_speed[1] * stream_speed[1]
        + stream_speed[2] * stream_speed[2]
    )
    holder_buffer = stream_speed[stream_heading]
    divided_pieces = [fluid_rho_value * holder_buffer]
    for entry_number in range(3):
        forcing_contribution = fluid_rho_value * stream_speed[entry_number] * holder_buffer
        if entry_number == stream_heading:
            forcing_contribution = forcing_contribution + thermo_stress_level
        divided_pieces.append(forcing_contribution)
    divided_pieces.append((overall_heat_work + thermo_stress_level) * holder_buffer)
    return jnp.stack(divided_pieces)


def fourth_diff(padded, along_axis, length):
    near_diff = lax.slice_in_dim(padded, 3, length + 3, axis=along_axis) - lax.slice_in_dim(
        padded, 1, length + 1, axis=along_axis
    )
    far_diff = lax.slice_in_dim(padded, 4, length + 4, axis=along_axis) - lax.slice_in_dim(
        padded, 0, length, axis=along_axis
    )
    return (8.0 * near_diff - far_diff) / 12.0


def filter_rows():
    n = AZIMUTH
    modes = np.arange(n // 2 + 1, dtype=np.float64)
    lag = np.arange(n)
    factor = np.where((modes == 0) | (modes == n // 2), 1.0, 2.0) / n
    table = np.cos((modes[:, None] * lag[None, :]) % n * (2.0 * np.pi / n))
    rows = np.zeros((CYCLES, 8, n), np.float32)
    for j in range(CYCLES):
        weight = np.exp(-((modes / (4.0 * (j + 1))) ** 8)) * factor
        h = weight @ table
        for r in range(8):
            rows[j, r] = np.roll(h, r)
    return rows


def pieces_of(value, count):
    out = []
    for _ in range(count - 1):
        part = value.astype(jnp.bfloat16)
        out.append(part)
        value = value - part.astype(jnp.float32)
    out.append(value.astype(jnp.bfloat16))
    return out


def dot_t(a, b):
    return lax.dot_general(a, b, (((1,), (1,)), ((), ())), preferred_element_type=jnp.float32)


def sums_kernel(count_ref, q_ref, cells_ref, bins_ref, amp_ref, out_ref):
    rows, lanes = q_ref.shape[1:]
    slots = cells_ref.shape[1]
    rho = q_ref[0]
    m1, m2, m3 = q_ref[1], q_ref[2], q_ref[3]
    kinetic = 0.5 * (m1 * (m1 / rho) + m2 * (m2 / rho) + m3 * (m3 / rho))
    excess = gas_factor * (q_ref[4] - kinetic) - ref_pressure
    parts = jnp.concatenate(pieces_of(excess.T, 3), axis=0)
    cells = cells_ref[...]
    row_hot = lax.broadcasted_iota(jnp.int32, (rows, slots), 0) == (cells >> 7)
    row_hot = jnp.where(row_hot, 1.0, 0.0).astype(jnp.bfloat16)
    picked = jnp.dot(parts, row_hot, preferred_element_type=jnp.float32)
    picked = picked[:lanes] + picked[lanes : 2 * lanes] + picked[2 * lanes :]
    lane_hot = lax.broadcasted_iota(jnp.int32, (lanes, slots), 0) == (cells & 127)
    sampled = jnp.sum(jnp.where(lane_hot, picked, 0.0), axis=0, keepdims=True)
    live = lax.broadcasted_iota(jnp.int32, (1, slots), 1) < count_ref[0]
    sampled = jnp.where(live, sampled, 0.0)
    owner_rows = lax.broadcasted_iota(jnp.int32, (16, slots), 0)
    rest_rows = lax.broadcasted_iota(jnp.int32, (64, slots), 0)

    def pair(i, carry):
        halves = []
        for top in range(2):
            o = top * 32 + i
            b = bins_ref[pl.ds(o, 1), :]
            contrib = sampled * amp_ref[pl.ds(o, 1), :]
            hit = owner_rows == ((b >> 1) & 15)
            left = jnp.concatenate(
                [
                    jnp.where(hit, part.astype(jnp.float32), 0.0).astype(jnp.bfloat16)
                    for part in pieces_of(contrib, 2)
                ],
                axis=0,
            )
            right = jnp.where(rest_rows == (((b & 1) << 5) | (b >> 5)), 1.0, 0.0).astype(
                jnp.bfloat16
            )
            both = dot_t(left, right)
            halves.append(both[:16] + both[16:])
        out_ref[:, pl.ds(i, 1), :] = jnp.concatenate(halves, axis=1).reshape(16, 1, 128)
        return carry

    lax.fori_loop(0, 32, pair, 0, unroll=4)


def reduce_kernel(p_ref, out_ref, got1, got2, rows2, send1, recv1, send2, recv2):
    ax, az = lax.axis_index("ax"), lax.axis_index("az")
    n_ax, n_az = 32, 16
    barrier = pltpu.get_barrier_semaphore()
    for r in range(1, n_az):
        pl.semaphore_signal(
            barrier, inc=1, device_id=(ax, lax.rem(az + r, n_az)), device_id_type=MESH
        )
    for r in range(1, n_ax):
        pl.semaphore_signal(
            barrier, inc=1, device_id=(lax.rem(ax + r, n_ax), az), device_id_type=MESH
        )
    pl.semaphore_wait(barrier, n_az - 1 + n_ax - 1)
    first = []
    for r in range(1, n_az):
        peer = lax.rem(az + r, n_az)
        copy = pltpu.make_async_remote_copy(
            src_ref=p_ref.at[peer],
            dst_ref=got1.at[r - 1],
            send_sem=send1.at[r - 1],
            recv_sem=recv1.at[r - 1],
            device_id=(ax, peer),
            device_id_type=MESH,
        )
        copy.start()
        first.append(copy)
    total = p_ref[az]
    for r in range(1, n_az):
        first[r - 1].wait_recv()
        total = total + got1[r - 1]
    turned = total.T
    rows2[...] = jnp.concatenate(
        [turned[(top * 2 + e) * 32 : (top * 2 + e) * 32 + 32] for e in range(2) for top in range(2)],
        axis=1,
    ).reshape(n_ax, 1, 128)
    second = []
    for r in range(1, n_ax):
        peer = lax.rem(ax + r, n_ax)
        copy = pltpu.make_async_remote_copy(
            src_ref=rows2.at[peer],
            dst_ref=got2.at[r - 1],
            send_sem=send2.at[r - 1],
            recv_sem=recv2.at[r - 1],
            device_id=(peer, az),
            device_id_type=MESH,
        )
        copy.start()
        second.append(copy)
    total = rows2[ax]
    for r in range(1, n_ax):
        second[r - 1].wait_recv()
        total = total + got2[r - 1]
    out_ref[...] = total
    for copy in first + second:
        copy.wait_send()


def filter_kernel(x_ref, h_ref, out_ref):
    h = h_ref[...]
    g = jnp.concatenate([h if k == 0 else pltpu.roll(h, 8 * k, 1) for k in range(16)], axis=0)
    g_hi, g_lo = pieces_of(g, 2)
    x = x_ref[...]
    lines = x.shape[0]
    turned = jnp.concatenate(
        [
            x if a == 0 else jnp.concatenate([x[:, 128 * a :], x[:, : 128 * a]], axis=1)
            for a in range(8)
        ],
        axis=0,
    )
    x_hi, x_lo = pieces_of(turned, 2)
    y = dot_t(x_hi, g_hi) + (dot_t(x_lo, g_hi) + dot_t(x_hi, g_lo))
    for a in range(8):
        out_ref[:, 128 * a : 128 * a + 128] = y[a * lines : (a + 1) * lines]


def on_device(conserved, panel_cells, panel_counts, time_bins, amplitudes):
    planes_dev = conserved.shape[1]
    sector = conserved.shape[2]
    radial_all = conserved.shape[3]
    slots = panel_cells.shape[0]
    vmem = pl.BlockSpec(memory_space=pltpu.VMEM)
    smem = pl.BlockSpec(memory_space=pltpu.SMEM)
    partial_signal = pl.pallas_call(
        sums_kernel,
        out_shape=jax.ShapeDtypeStruct((16, 32, 128), jnp.float32),
        in_specs=[smem] + [vmem] * 4,
        out_specs=vmem,
        name="sums",
    )(
        panel_counts,
        conserved.reshape(5, planes_dev * sector, radial_all),
        panel_cells.reshape(1, slots),
        time_bins.T,
        amplitudes.T,
    )
    signal = pl.pallas_call(
        reduce_kernel,
        out_shape=jax.ShapeDtypeStruct((1, 128), jnp.float32),
        in_specs=[vmem],
        out_specs=vmem,
        scratch_shapes=[
            pltpu.VMEM((15, 32, 128), jnp.float32),
            pltpu.VMEM((31, 1, 128), jnp.float32),
            pltpu.VMEM((32, 1, 128), jnp.float32),
            pltpu.SemaphoreType.DMA((15,)),
            pltpu.SemaphoreType.DMA((15,)),
            pltpu.SemaphoreType.DMA((31,)),
            pltpu.SemaphoreType.DMA((31,)),
        ],
        compiler_params=pltpu.CompilerParams(collective_id=0, has_side_effects=True),
        name="reduce",
    )(partial_signal)
    signal = signal.reshape(2, OBSERVERS).T

    primitive = primitives(conserved)
    radius = jnp.arange(radial_all).astype(jnp.float32) + 0.5
    dtheta = 2.0 * math.pi / AZIMUTH
    axial_flux = flux_along(primitive, 0)
    swirl_flux = flux_along(primitive, 2)
    padded_x = padded_2(axial_flux, (("ax", 1),), 2, False)
    padded_t = padded_2(swirl_flux, (("az", 2),), 2, True)
    radial_flux = flux_along(primitive, 1)
    padded_r = jnp.pad(radial_flux * radius, ((0, 0), (0, 0), (0, 0), (2, 2)))
    tendency = -fourth_diff(padded_x, 1, planes_dev)
    tendency = tendency - fourth_diff(padded_r, 3, radial_all) / radius
    tendency = tendency - fourth_diff(padded_t, 2, sector) / (radius * dtheta)
    fluid_rho_value = primitive[0]
    radial_vel = primitive[2]
    swirl_vel = primitive[3]
    thermo_stress_level = primitive[4]
    zeros_field = jnp.zeros_like(fluid_rho_value)
    source = jnp.stack(
        [
            zeros_field,
            zeros_field,
            (thermo_stress_level + fluid_rho_value * swirl_vel * swirl_vel) / radius,
            -fluid_rho_value * radial_vel * swirl_vel / radius,
            zeros_field,
        ]
    )
    raw_section = conserved + time_step * (tendency + source)
    inner = raw_section[..., :CYCLES].reshape(5, 2, planes_dev // 2, sector, CYCLES)
    lines = jnp.transpose(inner, (4, 1, 0, 2, 3)).reshape(16, 20, sector)
    lines = lax.all_to_all(lines, "az", split_axis=0, concat_axis=0, tiled=True)
    lines = jnp.transpose(lines, (1, 0, 2)).reshape(20, AZIMUTH)
    lines = jnp.pad(lines, ((0, 4), (0, 0)))
    rows = lax.dynamic_index_in_dim(
        jnp.asarray(filter_rows()), lax.axis_index("az") // 2, 0, keepdims=False
    )
    smooth = pl.pallas_call(
        filter_kernel,
        out_shape=jax.ShapeDtypeStruct((24, AZIMUTH), jnp.float32),
        in_specs=[vmem] * 2,
        out_specs=vmem,
        name="filter",
    )(lines, rows)
    smooth = jnp.transpose(smooth[:20].reshape(20, 16, sector), (1, 0, 2))
    smooth = lax.all_to_all(smooth, "az", split_axis=0, concat_axis=0, tiled=True)
    filtered = jnp.transpose(
        smooth.reshape(CYCLES, 2, 5, planes_dev // 2, sector), (2, 1, 3, 4, 0)
    ).reshape(5, planes_dev, sector, CYCLES)
    section = jnp.concatenate([filtered, raw_section[..., CYCLES:]], axis=3)
    return (section, signal)


def solution(mesh):
    placed = (
        P(None, "ax", "az", None),
        P(("ax", "az")),
        P(("ax", "az")),
        P(("ax", "az"), None),
        P(("ax", "az"), None),
    )
    return jax.shard_map(
        on_device,
        mesh=mesh,
        in_specs=placed,
        out_specs=(P(None, "ax", "az", None), P(None, ("ax", "az"))),
        check_vma=False,
    )
```

```python
import math

import jax
import jax.numpy as jnp
import numpy as np
from jax import lax
from jax.experimental import pallas as pl
from jax.experimental.pallas import tpu as pltpu
from jax.sharding import PartitionSpec as P

AZIMUTH = 1024
CYCLES = 8
OBSERVERS = 64
BINS = 1024
MESH = pl.DeviceIdType.MESH

gas_factor = 0.4
time_step = 0.02
ref_pressure = 0.95


def filter_rows():
    n = AZIMUTH
    modes = np.arange(n // 2 + 1, dtype=np.float64)
    lag = np.arange(n)
    factor = np.where((modes == 0) | (modes == n // 2), 1.0, 2.0) / n
    table = np.cos((modes[:, None] * lag[None, :]) % n * (2.0 * np.pi / n))
    rows = np.zeros((CYCLES, 8, n), np.float32)
    for j in range(CYCLES):
        weight = np.exp(-((modes / (4.0 * (j + 1))) ** 8)) * factor
        h = weight @ table
        for r in range(8):
            rows[j, r] = np.roll(h, r)
    return rows


def pieces_of(value, count):
    out = []
    for _ in range(count - 1):
        part = value.astype(jnp.bfloat16)
        out.append(part)
        value = value - part.astype(jnp.float32)
    out.append(value.astype(jnp.bfloat16))
    return out


def dot_t(a, b):
    return lax.dot_general(a, b, (((1,), (1,)), ((), ())), preferred_element_type=jnp.float32)


def axis_ring(n, me, r):
    return lax.rem(me + r, n)


def step_kernel(
    count_ref,
    cells_ref,
    q_hbm,
    bins_hbm,
    amp_hbm,
    h_hbm,
    out_ref,
    sig_ref,
    q,
    bins,
    amp,
    h,
    axial,
    swirl,
    excess,
    edge_out,
    edge_in,
    inner,
    lines_out,
    lines_in,
    smooth_out,
    smooth_in,
    sums,
    sums_in,
    rows,
    rows_in,
    g_hi,
    g_lo,
    load_sem,
    near_send,
    near_recv,
    sums_send,
    sums_recv,
    rows_send,
    rows_recv,
    lines_send,
    lines_recv,
    smooth_send,
    smooth_recv,
):
    n_ax, n_az = 32, 16
    ax, az = lax.axis_index("ax"), lax.axis_index("az")

    def remote(source, target, send, recv, ax_to, az_to):
        return pltpu.make_async_remote_copy(
            src_ref=source,
            dst_ref=target,
            send_sem=send,
            recv_sem=recv,
            device_id=(ax_to, az_to),
            device_id_type=MESH,
        )

    loads = [
        pltpu.make_async_copy(q_hbm, q, load_sem.at[0]),
        pltpu.make_async_copy(bins_hbm, bins, load_sem.at[1]),
        pltpu.make_async_copy(amp_hbm, amp, load_sem.at[2]),
        pltpu.make_async_copy(h_hbm.at[lax.rem(az, CYCLES)], h, load_sem.at[3]),
    ]
    for copy in loads:
        copy.start()
    barrier = pltpu.get_barrier_semaphore()
    for r in range(1, n_ax):
        pl.semaphore_signal(
            barrier, inc=1, device_id=(axis_ring(n_ax, ax, r), az), device_id_type=MESH
        )
    for r in range(1, n_az):
        pl.semaphore_signal(
            barrier, inc=1, device_id=(ax, axis_ring(n_az, az, r)), device_id_type=MESH
        )

    lane = lax.broadcasted_iota(jnp.int32, (1, 128), 1)
    radius = lane.astype(jnp.float32) + 0.5
    over_r = 1.0 / radius
    step = jnp.float32(time_step)
    dtheta = 2.0 * math.pi / AZIMUTH
    near = (8.0 / 12.0) * step * over_r
    far = (1.0 / 12.0) * step * over_r
    plus_1 = jnp.where(lane < 127, -near, 0.0)
    minus_1 = jnp.where(lane > 0, near, 0.0)
    plus_2 = jnp.where(lane < 126, far, 0.0)
    minus_2 = jnp.where(lane > 1, -far, 0.0)
    swirl_gain = (-1.0 / 12.0) * step / (radius * dtheta)
    axial_gain = -time_step / 12.0

    loads[0].wait()

    def local(i, carry):
        p = i // 4
        at = pl.multiple_of((i % 4) * 16, 16)
        part = pl.ds(at, 16)
        q0, q1, q2, q3, q4 = [q[f, p, part, :] for f in range(5)]
        over = 1.0 / q0
        u, v, w = q1 * over, q2 * over, q3 * over
        pressure = gas_factor * (q4 - 0.5 * (q1 * u + q2 * v + q3 * w))
        excess[pl.ds(pl.multiple_of(i * 16, 16), 16), :] = pressure - ref_pressure
        total = q4 + pressure
        for f, value in enumerate((q1, q1 * u + pressure, q2 * u, q3 * u, total * u)):
            axial[p + 2, f, part, :] = value
        into = pl.ds(at + 8, 16)
        q3w = q3 * w
        for f, value in enumerate((q3, q1 * w, q2 * w, q3w + pressure, total * w)):
            swirl[f, p, into, :] = value
        q3v = q3 * v
        force = step * over_r
        old = (q0, q1, q2 + force * (pressure + q3w), q3 - force * q3v, q4)
        for f, value in enumerate((q2, q1 * v, q2 * v + pressure, q3v, total * v)):
            value = value * radius
            out_ref[f, p, part, :] = (
                old[f]
                + plus_1 * pltpu.roll(value, 127, 1)
                + minus_1 * pltpu.roll(value, 1, 1)
                + plus_2 * pltpu.roll(value, 126, 1)
                + minus_2 * pltpu.roll(value, 2, 1)
            )
        return carry

    lax.fori_loop(0, 32, local, 0, unroll=2)

    for f in range(5):
        for r in range(2):
            edge_out[0, f, r] = swirl[f, :, 8 + r, :]
            edge_out[1, f, r] = swirl[f, :, 70 + r, :]

    def turn_axial(f, carry):
        for a in range(4):
            tile = jnp.concatenate([axial[2 * a + 2, f], axial[2 * a + 3, f]], axis=0)
            inner[a + 1, f] = tile.T[:8]
        return carry

    lax.fori_loop(0, 5, turn_axial, 0)

    @pl.when(ax == 0)
    def _():
        inner[0] = jnp.zeros_like(inner[0])
        axial[0:2] = jnp.zeros((2, 5, 64, 128), jnp.float32)

    @pl.when(ax == n_ax - 1)
    def _():
        inner[5] = jnp.zeros_like(inner[5])
        axial[10:12] = jnp.zeros((2, 5, 64, 128), jnp.float32)

    slots = cells_ref.shape[1]
    parts = jnp.concatenate(pieces_of(excess[...].T, 3), axis=0)
    cells = cells_ref[...]
    row_hot = lax.broadcasted_iota(jnp.int32, (512, slots), 0) == (cells >> 7)
    row_hot = jnp.where(row_hot, 1.0, 0.0).astype(jnp.bfloat16)
    picked = jnp.dot(parts, row_hot, preferred_element_type=jnp.float32)
    picked = picked[:128] + picked[128:256] + picked[256:]
    lane_hot = lax.broadcasted_iota(jnp.int32, (128, slots), 0) == (cells & 127)
    sampled = jnp.sum(jnp.where(lane_hot, picked, 0.0), axis=0, keepdims=True)
    live = lax.broadcasted_iota(jnp.int32, (1, slots), 1) < count_ref[0]
    sampled = jnp.where(live, sampled, 0.0)
    owner_rows = lax.broadcasted_iota(jnp.int32, (16, slots), 0)
    rest_rows = lax.broadcasted_iota(jnp.int32, (64, slots), 0)
    loads[1].wait()
    loads[2].wait()

    def pair(i, carry):
        halves = []
        for top in range(2):
            o = top * 32 + i
            b = bins[pl.ds(o, 1), :]
            contrib = sampled * amp[pl.ds(o, 1), :]
            hit = owner_rows == ((b >> 1) & 15)
            left = jnp.concatenate(
                [
                    jnp.where(hit, piece.astype(jnp.float32), 0.0).astype(jnp.bfloat16)
                    for piece in pieces_of(contrib, 2)
                ],
                axis=0,
            )
            right = jnp.where(rest_rows == (((b & 1) << 5) | (b >> 5)), 1.0, 0.0).astype(
                jnp.bfloat16
            )
            both = dot_t(left, right)
            halves.append(both[:16] + both[16:])
        sums[:, pl.ds(i, 1), :] = jnp.concatenate(halves, axis=1).reshape(16, 1, 128)
        return carry

    lax.fori_loop(0, 32, pair, 0, unroll=4)

    pl.semaphore_wait(barrier, n_ax - 1 + n_az - 1)
    below, above = axis_ring(n_ax, ax, n_ax - 1), axis_ring(n_ax, ax, 1)
    left_az, right_az = axis_ring(n_az, az, n_az - 1), axis_ring(n_az, az, 1)
    edge_low = remote(
        edge_out.at[0], edge_in.at[1], near_send.at[0], near_recv.at[0], ax, left_az
    )
    edge_high = remote(
        edge_out.at[1], edge_in.at[0], near_send.at[1], near_recv.at[1], ax, right_az
    )
    inner_down = remote(inner.at[1], inner.at[5], near_send.at[2], near_recv.at[2], below, az)
    inner_up = remote(inner.at[4], inner.at[0], near_send.at[3], near_recv.at[3], above, az)
    halo_down = remote(
        axial.at[pl.ds(2, 2)],
        axial.at[pl.ds(10, 2)],
        near_send.at[4],
        near_recv.at[4],
        below,
        az,
    )
    halo_up = remote(
        axial.at[pl.ds(8, 2)],
        axial.at[pl.ds(0, 2)],
        near_send.at[5],
        near_recv.at[5],
        above,
        az,
    )
    edge_low.start()
    edge_high.start()

    @pl.when(ax > 0)
    def _():
        inner_down.start()
        halo_down.start()

    @pl.when(ax < n_ax - 1)
    def _():
        inner_up.start()
        halo_up.start()

    sums_copies = []
    for r in range(1, n_az):
        peer = axis_ring(n_az, az, r)
        copy = remote(
            sums.at[peer], sums_in.at[r - 1], sums_send.at[r - 1], sums_recv.at[r - 1], ax, peer
        )
        copy.start()
        sums_copies.append(copy)

    loads[3].wait()
    first = h[...]
    for k in range(16):
        g = first if k == 0 else pltpu.roll(first, 8 * k, 1)
        hi = g.astype(jnp.bfloat16).astype(jnp.float32)
        g_hi[8 * k : 8 * k + 8] = hi
        g_lo[8 * k : 8 * k + 8] = g - hi

    edge_low.wait_recv()
    edge_high.wait_recv()
    for f in range(5):
        for r in range(2):
            swirl[f, :, 6 + r, :] = edge_in[0, f, r]
            swirl[f, :, 72 + r, :] = edge_in[1, f, r]

    def around(p, carry):
        for f in range(5):
            out_ref[f, p] = out_ref[f, p] + swirl_gain * (
                8.0 * (swirl[f, p, 9:73, :] - swirl[f, p, 7:71, :])
                - (swirl[f, p, 10:74, :] - swirl[f, p, 6:70, :])
            )
        return carry

    lax.fori_loop(0, 8, around, 0)

    @pl.when(ax < n_ax - 1)
    def _():
        inner_down.wait_recv()

    @pl.when(ax > 0)
    def _():
        inner_up.wait_recv()

    upper = lane >= 64
    for d in range(n_az):
        lines_out[d, 8:16, :] = jnp.zeros((8, 128), jnp.float32)

    def turn_lines(f, carry):
        for a in range(4):
            tile = jnp.concatenate([out_ref[f, 2 * a], out_ref[f, 2 * a + 1]], axis=0)
            before, now, after = inner[a, f], inner[a + 1, f], inner[a + 2, f]
            next_1 = pltpu.roll(jnp.where(upper, now, after), 64, 1)
            last_1 = pltpu.roll(jnp.where(upper, before, now), 64, 1)
            line = tile.T[:8] + axial_gain * (8.0 * (next_1 - last_1) - (after - before))
            lines_out[
                pl.ds((a // 2) * 8, 8), pl.ds(f * 2 + a % 2, 1), :
            ] = line.reshape(8, 1, 128)
        return carry

    lax.fori_loop(0, 5, turn_lines, 0)
    lines_copies = []
    for r in range(1, n_az):
        peer = axis_ring(n_az, az, r)
        copy = remote(
            lines_out.at[peer], lines_in.at[az], lines_send.at[r - 1], lines_recv.at[r - 1], ax, peer
        )
        copy.start()
        lines_copies.append(copy)
    lines_in[az] = lines_out[az]

    total = sums[az]
    for r in range(1, n_az):
        sums_copies[r - 1].wait_recv()
        total = total + sums_in[r - 1]
    turned = total.T
    rows[...] = jnp.concatenate(
        [turned[(top * 2 + e) * 32 : (top * 2 + e) * 32 + 32] for e in range(2) for top in range(2)],
        axis=1,
    ).reshape(n_ax, 1, 128)
    rows_copies = []
    for r in range(1, n_ax):
        peer = axis_ring(n_ax, ax, r)
        copy = remote(
            rows.at[peer], rows_in.at[r - 1], rows_send.at[r - 1], rows_recv.at[r - 1], peer, az
        )
        copy.start()
        rows_copies.append(copy)

    @pl.when(ax < n_ax - 1)
    def _():
        halo_down.wait_recv()

    @pl.when(ax > 0)
    def _():
        halo_up.wait_recv()

    def along(p, carry):
        for f in range(5):
            out_ref[f, p] = out_ref[f, p] + axial_gain * (
                8.0 * (axial[p + 3, f] - axial[p + 1, f]) - (axial[p + 4, f] - axial[p, f])
            )
        return carry

    lax.fori_loop(0, 8, along, 0)

    for copy in lines_copies:
        copy.wait_recv()
    low, high = [], []
    for s in range(0, n_az, 2):
        one, two = lines_in[s], lines_in[s + 1]
        low.append(jnp.where(upper, pltpu.roll(two, 64, 1), one))
        high.append(jnp.where(upper, two, pltpu.roll(one, 64, 1)))
    x = jnp.concatenate(
        [jnp.concatenate(low, axis=1), jnp.concatenate(high, axis=1)], axis=0
    )
    turns = jnp.concatenate(
        [
            x if a == 0 else jnp.concatenate([x[:, 128 * a :], x[:, : 128 * a]], axis=1)
            for a in range(8)
        ],
        axis=0,
    )
    x_hi, x_lo = pieces_of(turns, 2)
    k_hi, k_lo = g_hi[...].astype(jnp.bfloat16), g_lo[...].astype(jnp.bfloat16)
    y = dot_t(x_hi, k_hi) + (dot_t(x_lo, k_hi) + dot_t(x_hi, k_lo))
    for a in range(8):
        one, two = y[32 * a : 32 * a + 16], y[32 * a + 16 : 32 * a + 32]
        smooth_out[2 * a] = jnp.where(upper, pltpu.roll(two, 64, 1), one)
        smooth_out[2 * a + 1] = jnp.where(upper, two, pltpu.roll(one, 64, 1))
    smooth_copies = []
    for r in range(1, n_az):
        peer = axis_ring(n_az, az, r)
        copy = remote(
            smooth_out.at[peer],
            smooth_in.at[az],
            smooth_send.at[r - 1],
            smooth_recv.at[r - 1],
            ax,
            peer,
        )
        copy.start()
        smooth_copies.append(copy)
    smooth_in[az] = smooth_out[az]
    for copy in smooth_copies:
        copy.wait_recv()
    cycles = lane < 8

    def turn_back(f, carry):
        for a in range(4):
            line = smooth_in[
                pl.ds((a // 2) * 8, 8), pl.ds(f * 2 + a % 2, 1), :
            ].reshape(8, 128)
            tile = jnp.concatenate([line, jnp.zeros((120, 128), jnp.float32)], axis=0).T
            for b in range(2):
                out_ref[f, 2 * a + b] = jnp.where(
                    cycles, tile[64 * b : 64 * b + 64], out_ref[f, 2 * a + b]
                )
        return carry

    lax.fori_loop(0, 5, turn_back, 0)
    total = rows[ax]
    for r in range(1, n_ax):
        rows_copies[r - 1].wait_recv()
        total = total + rows_in[r - 1]
    sig_ref[...] = total

    for copy in [edge_low, edge_high] + sums_copies + lines_copies + rows_copies + smooth_copies:
        copy.wait_send()

    @pl.when(ax > 0)
    def _():
        inner_down.wait_send()
        halo_down.wait_send()

    @pl.when(ax < n_ax - 1)
    def _():
        inner_up.wait_send()
        halo_up.wait_send()


def on_device(conserved, panel_cells, panel_counts, time_bins, amplitudes):
    f32 = jnp.float32
    vmem = pl.BlockSpec(memory_space=pltpu.VMEM)
    smem = pl.BlockSpec(memory_space=pltpu.SMEM)
    hbm = pl.BlockSpec(memory_space=pl.ANY)
    dma = pltpu.SemaphoreType.DMA
    section, signal = pl.pallas_call(
        step_kernel,
        out_shape=(
            jax.ShapeDtypeStruct(conserved.shape, f32),
            jax.ShapeDtypeStruct((1, 128), f32),
        ),
        in_specs=[smem, vmem, hbm, hbm, hbm, hbm],
        out_specs=(vmem, vmem),
        scratch_shapes=[
            pltpu.VMEM((5, 8, 64, 128), f32),
            pltpu.VMEM((64, 512), jnp.int32),
            pltpu.VMEM((64, 512), f32),
            pltpu.VMEM((8, 1024), f32),
            pltpu.VMEM((12, 5, 64, 128), f32),
            pltpu.VMEM((5, 8, 80, 128), f32),
            pltpu.VMEM((512, 128), f32),
            pltpu.VMEM((2, 5, 2, 8, 128), f32),
            pltpu.VMEM((2, 5, 2, 8, 128), f32),
            pltpu.VMEM((6, 5, 8, 128), f32),
            pltpu.VMEM((16, 16, 128), f32),
            pltpu.VMEM((16, 16, 128), f32),
            pltpu.VMEM((16, 16, 128), f32),
            pltpu.VMEM((16, 16, 128), f32),
            pltpu.VMEM((16, 32, 128), f32),
            pltpu.VMEM((15, 32, 128), f32),
            pltpu.VMEM((32, 1, 128), f32),
            pltpu.VMEM((31, 1, 128), f32),
            pltpu.VMEM((128, 1024), f32),
            pltpu.VMEM((128, 1024), f32),
            dma((4,)),
            dma((6,)),
            dma((6,)),
            dma((15,)),
            dma((15,)),
            dma((31,)),
            dma((31,)),
            dma((15,)),
            dma((15,)),
            dma((15,)),
            dma((15,)),
        ],
        compiler_params=pltpu.CompilerParams(collective_id=0, has_side_effects=True),
        name="step",
    )(
        panel_counts,
        panel_cells.reshape(1, panel_cells.shape[0]),
        conserved,
        time_bins.T,
        amplitudes.T,
        jnp.asarray(filter_rows()),
    )
    return (section, signal.reshape(2, OBSERVERS).T)


def solution(mesh):
    placed = (
        P(None, "ax", "az", None),
        P(("ax", "az")),
        P(("ax", "az")),
        P(("ax", "az"), None),
        P(("ax", "az"), None),
    )
    return jax.shard_map(
        on_device,
        mesh=mesh,
        in_specs=placed,
        out_specs=(P(None, "ax", "az", None), P(None, ("ax", "az"))),
        check_vma=False,
    )
```

```python
import math

import jax
import jax.numpy as jnp
import numpy as np
from jax import lax
from jax.experimental import pallas as pl
from jax.experimental.pallas import tpu as pltpu
from jax.sharding import PartitionSpec as P

AZIMUTH = 1024
CYCLES = 8
OBSERVERS = 64
BINS = 1024
MESH = pl.DeviceIdType.MESH

gas_factor = 0.4
time_step = 0.02
ref_pressure = 0.95


def filter_rows():
    n = AZIMUTH
    modes = np.arange(n // 2 + 1, dtype=np.float64)
    lag = np.arange(n)
    factor = np.where((modes == 0) | (modes == n // 2), 1.0, 2.0) / n
    table = np.cos((modes[:, None] * lag[None, :]) % n * (2.0 * np.pi / n))
    rows = np.zeros((CYCLES, 8, n), np.float32)
    for j in range(CYCLES):
        weight = np.exp(-((modes / (4.0 * (j + 1))) ** 8)) * factor
        h = weight @ table
        for r in range(8):
            rows[j, r] = np.roll(h, r)
    return rows


def pieces_of(value, count):
    out = []
    for _ in range(count - 1):
        part = value.astype(jnp.bfloat16)
        out.append(part)
        value = value - part.astype(jnp.float32)
    out.append(value.astype(jnp.bfloat16))
    return out


def dot_t(a, b):
    return lax.dot_general(a, b, (((1,), (1,)), ((), ())), preferred_element_type=jnp.float32)


def axis_ring(n, me, r):
    return lax.rem(me + r, n)


def step_kernel(
    count,
    cells_hbm,
    q_hbm,
    bins_hbm,
    amp_hbm,
    h_hbm,
    out_ref,
    sig_ref,
    raw,
    cells_ref,
    q,
    bins,
    amp,
    h,
    axial,
    swirl,
    excess,
    edge_out,
    edge_in,
    inner,
    lines_out,
    lines_in,
    smooth_out,
    smooth_in,
    sums,
    sums_in,
    rows,
    rows_in,
    g_hi,
    g_lo,
    load_sem,
    plane_sem,
    near_send,
    near_recv,
    bulk_send,
    bulk_recv,
):
    n_ax, n_az = 32, 16
    ax, az = lax.axis_index("ax"), lax.axis_index("az")

    def remote(source, target, send, recv, ax_to, az_to):
        return pltpu.make_async_remote_copy(
            src_ref=source,
            dst_ref=target,
            send_sem=send,
            recv_sem=recv,
            device_id=(ax_to, az_to),
            device_id_type=MESH,
        )

    loads = [
        pltpu.make_async_copy(cells_hbm, cells_ref, load_sem.at[0]),
        pltpu.make_async_copy(bins_hbm, bins, load_sem.at[1]),
        pltpu.make_async_copy(amp_hbm, amp, load_sem.at[2]),
        pltpu.make_async_copy(h_hbm.at[lax.rem(az, CYCLES)], h, load_sem.at[3]),
    ]

    def plane_load(p):
        return pltpu.make_async_copy(q_hbm.at[:, p], q.at[:, p], plane_sem.at[p])

    for p in range(8):
        plane_load(p).start()
    for copy in loads:
        copy.start()
    barrier = pltpu.get_barrier_semaphore()
    for k in range(1, n_ax):
        r = n_ax // 2 + (k // 2 if k % 2 == 0 else -(k // 2))
        pl.semaphore_signal(
            barrier, inc=1, device_id=(axis_ring(n_ax, ax, r), az), device_id_type=MESH
        )
    for r in range(1, n_az):
        pl.semaphore_signal(
            barrier, inc=1, device_id=(ax, axis_ring(n_az, az, r)), device_id_type=MESH
        )

    lane = lax.broadcasted_iota(jnp.int32, (1, 128), 1)
    radius = lane.astype(jnp.float32) + 0.5
    over_r = 1.0 / radius
    step = jnp.float32(time_step)
    dtheta = 2.0 * math.pi / AZIMUTH
    near = (8.0 / 12.0) * step * over_r
    far = (1.0 / 12.0) * step * over_r
    plus_1 = jnp.where(lane < 127, -near, 0.0)
    minus_1 = jnp.where(lane > 0, near, 0.0)
    plus_2 = jnp.where(lane < 126, far, 0.0)
    minus_2 = jnp.where(lane > 1, -far, 0.0)
    swirl_gain = (-1.0 / 12.0) * step / (radius * dtheta)
    axial_gain = -time_step / 12.0


    def local(p, carry):
        plane_load(p).wait()
        for at in range(0, 64, 16):
            part = pl.ds(at, 16)
            q0, q1, q2, q3, q4 = [q[f, p, part, :] for f in range(5)]
            over = 1.0 / q0
            u, v, w = q1 * over, q2 * over, q3 * over
            pressure = gas_factor * (q4 - 0.5 * (q1 * u + q2 * v + q3 * w))
            excess[pl.ds(pl.multiple_of(p * 64 + at, 16), 16), :] = pressure - ref_pressure
            total = q4 + pressure
            for f, value in enumerate((q1, q1 * u + pressure, q2 * u, q3 * u, total * u)):
                axial[p + 2, f, part, :] = value
            into = pl.ds(at + 8, 16)
            q3w = q3 * w
            for f, value in enumerate((q3, q1 * w, q2 * w, q3w + pressure, total * w)):
                swirl[f, p, into, :] = value
            q3v = q3 * v
            force = step * over_r
            old = (q0, q1, q2 + force * (pressure + q3w), q3 - force * q3v, q4)
            for f, value in enumerate((q2, q1 * v, q2 * v + pressure, q3v, total * v)):
                value = value * radius
                raw[f, p, part, :] = (
                    old[f]
                    + plus_1 * pltpu.roll(value, 127, 1)
                    + minus_1 * pltpu.roll(value, 1, 1)
                    + plus_2 * pltpu.roll(value, 126, 1)
                    + minus_2 * pltpu.roll(value, 2, 1)
                )
        return carry

    lax.fori_loop(0, 8, local, 0)

    for f in range(5):
        for r in range(2):
            edge_out[0, f, r] = swirl[f, :, 8 + r, :]
            edge_out[1, f, r] = swirl[f, :, 70 + r, :]

    @pl.when(ax == 0)
    def _():
        inner[0] = jnp.zeros_like(inner[0])
        axial[0:2] = jnp.zeros((2, 5, 64, 128), jnp.float32)

    @pl.when(ax == n_ax - 1)
    def _():
        inner[5] = jnp.zeros_like(inner[5])
        axial[10:12] = jnp.zeros((2, 5, 64, 128), jnp.float32)

    slots = cells_ref.shape[1]
    loads[0].wait()
    parts = jnp.concatenate(pieces_of(excess[...].T, 3), axis=0)
    cells = cells_ref[...]
    row_hot = lax.broadcasted_iota(jnp.int32, (512, slots), 0) == (cells >> 7)
    row_hot = jnp.where(row_hot, 1.0, 0.0).astype(jnp.bfloat16)
    picked = jnp.dot(parts, row_hot, preferred_element_type=jnp.float32)
    picked = picked[:128] + picked[128:256] + picked[256:]
    lane_hot = lax.broadcasted_iota(jnp.int32, (128, slots), 0) == (cells & 127)
    sampled = jnp.sum(jnp.where(lane_hot, picked, 0.0), axis=0, keepdims=True)
    live = lax.broadcasted_iota(jnp.int32, (1, slots), 1) < count[0]
    sampled = jnp.where(live, sampled, 0.0)
    sixteen = lax.broadcasted_iota(jnp.int32, (16, slots), 0)
    ladder = [(sixteen + 16 * k).astype(jnp.float32).astype(jnp.bfloat16) for k in range(4)]
    one, none = jnp.bfloat16(1.0), jnp.bfloat16(0.0)

    def spread(value, k):
        return jnp.broadcast_to(value[k : k + 1], (16, slots)).astype(jnp.bfloat16)

    loads[1].wait()
    loads[2].wait()

    def group(i, carry):
        ready = []
        for top in range(2):
            at = pl.ds(pl.multiple_of(top * 32 + i * 8, 8), 8)
            b = bins[at, :]
            contrib = sampled * amp[at, :]
            main = contrib.astype(jnp.bfloat16).astype(jnp.float32)
            owner = ((b >> 1) & 15).astype(jnp.float32)
            rest = (((b & 1) << 5) | (b >> 5)).astype(jnp.float32)
            ready.append((main, contrib - main, owner, rest))
        for k in range(8):
            halves = []
            for main, left_over, owner, rest in ready:
                hit = spread(owner, k) == ladder[0]
                left = jnp.concatenate(
                    [jnp.where(hit, spread(part, k), none) for part in (main, left_over)], axis=0
                )
                place = spread(rest, k)
                right = jnp.concatenate(
                    [jnp.where(place == rung, one, none) for rung in ladder], axis=0
                )
                both = dot_t(left, right)
                halves.append(both[:16] + both[16:])
            sums[:, pl.ds(i * 8 + k, 1), :] = jnp.concatenate(halves, axis=1).reshape(16, 1, 128)
        return carry

    lax.fori_loop(0, 2, group, 0)

    pl.semaphore_wait(barrier, n_ax - 1 + n_az - 1)
    below, above = axis_ring(n_ax, ax, n_ax - 1), axis_ring(n_ax, ax, 1)
    left_az, right_az = axis_ring(n_az, az, n_az - 1), axis_ring(n_az, az, 1)
    edge_low = remote(
        edge_out.at[0], edge_in.at[1], near_send.at[0], near_recv.at[0], ax, left_az
    )
    edge_high = remote(
        edge_out.at[1], edge_in.at[0], near_send.at[1], near_recv.at[1], ax, right_az
    )
    inner_down = remote(inner.at[1], inner.at[5], near_send.at[2], near_recv.at[2], below, az)
    inner_up = remote(inner.at[4], inner.at[0], near_send.at[3], near_recv.at[3], above, az)
    halo_down = remote(
        axial.at[pl.ds(2, 2)],
        axial.at[pl.ds(10, 2)],
        near_send.at[4],
        near_recv.at[4],
        below,
        az,
    )
    halo_up = remote(
        axial.at[pl.ds(8, 2)],
        axial.at[pl.ds(0, 2)],
        near_send.at[5],
        near_recv.at[5],
        above,
        az,
    )
    edge_low.start()
    edge_high.start()
    def turn_axial(f, carry):
        for a in range(4):
            tile = jnp.concatenate([axial[2 * a + 2, f], axial[2 * a + 3, f]], axis=0)
            inner[a + 1, f] = tile.T[:8]
        return carry

    lax.fori_loop(0, 5, turn_axial, 0)


    @pl.when(ax > 0)
    def _():
        inner_down.start()

    @pl.when(ax < n_ax - 1)
    def _():
        inner_up.start()

    @pl.when(ax > 0)
    def _():
        halo_down.start()

    @pl.when(jnp.logical_and(ax < n_ax - 1, ax != n_ax // 2 - 1))
    def _():
        halo_up.start()

    lax.fori_loop(2, 4, group, 0)
    for r in range(1, n_az):
        peer = axis_ring(n_az, az, r)
        remote(sums.at[peer], sums_in.at[r - 1], bulk_send.at[0], bulk_recv.at[0], ax, peer).start()
    all_sums = remote(
        sums.at[pl.ds(0, 15)], sums_in, bulk_send.at[0], bulk_recv.at[0], ax, right_az
    )

    loads[3].wait()
    first = h[...]
    for k in range(16):
        g = first if k == 0 else pltpu.roll(first, 8 * k, 1)
        hi = g.astype(jnp.bfloat16).astype(jnp.float32)
        g_hi[8 * k : 8 * k + 8] = hi
        g_lo[8 * k : 8 * k + 8] = g - hi

    edge_low.wait_recv()
    edge_high.wait_recv()
    for f in range(5):
        for r in range(2):
            swirl[f, :, 6 + r, :] = edge_in[0, f, r]
            swirl[f, :, 72 + r, :] = edge_in[1, f, r]

    def around(p, carry):
        for f in range(5):
            raw[f, p] = raw[f, p] + swirl_gain * (
                8.0 * (swirl[f, p, 9:73, :] - swirl[f, p, 7:71, :])
                - (swirl[f, p, 10:74, :] - swirl[f, p, 6:70, :])
            )
        return carry

    lax.fori_loop(0, 8, around, 0)

    @pl.when(ax < n_ax - 1)
    def _():
        inner_down.wait_recv()

    @pl.when(ax > 0)
    def _():
        inner_up.wait_recv()

    upper = lane >= 64
    for d in range(n_az):
        lines_out[d, 8:16, :] = jnp.zeros((8, 128), jnp.float32)
    lines_out = lines_out

    def turn_lines(f, carry):
        for a in range(4):
            tile = jnp.concatenate([raw[f, 2 * a], raw[f, 2 * a + 1]], axis=0)
            before, now, after = inner[a, f], inner[a + 1, f], inner[a + 2, f]
            next_1 = pltpu.roll(jnp.where(upper, now, after), 64, 1)
            last_1 = pltpu.roll(jnp.where(upper, before, now), 64, 1)
            line = tile.T[:8] + axial_gain * (8.0 * (next_1 - last_1) - (after - before))
            lines_out[
                pl.ds((a // 2) * 8, 8), pl.ds(f * 2 + a % 2, 1), :
            ] = line.reshape(8, 1, 128)
        return carry

    lax.fori_loop(0, 5, turn_lines, 0)
    for r in range(1, n_az):
        peer = axis_ring(n_az, az, r)
        remote(
            lines_out.at[peer], lines_in.at[az], bulk_send.at[1], bulk_recv.at[1], ax, peer
        ).start()
    most = pl.ds(0, 15)
    all_lines = remote(
        lines_out.at[most], lines_in.at[most], bulk_send.at[1], bulk_recv.at[1], ax, right_az
    )

    lines_in[az] = lines_out[az]

    all_sums.wait_recv()
    total = sums[az]
    for r in range(1, n_az):
        total = total + sums_in[r - 1]
    turned = total.T
    rows[...] = jnp.concatenate(
        [turned[(top * 2 + e) * 32 : (top * 2 + e) * 32 + 32] for e in range(2) for top in range(2)],
        axis=1,
    ).reshape(n_ax, 1, 128)
    for r in range(1, n_ax):
        peer = axis_ring(n_ax, ax, r)
        remote(rows.at[peer], rows_in.at[r - 1], bulk_send.at[2], bulk_recv.at[2], peer, az).start()
    all_rows = remote(
        rows.at[pl.ds(0, 31)], rows_in, bulk_send.at[2], bulk_recv.at[2], above, az
    )

    @pl.when(ax == n_ax // 2 - 1)
    def _():
        halo_up.start()

    all_lines.wait_recv()
    low, high = [], []
    for s in range(0, n_az, 2):
        one, two = lines_in[s], lines_in[s + 1]
        low.append(jnp.where(upper, pltpu.roll(two, 64, 1), one))
        high.append(jnp.where(upper, two, pltpu.roll(one, 64, 1)))
    x = jnp.concatenate(
        [jnp.concatenate(low, axis=1), jnp.concatenate(high, axis=1)], axis=0
    )
    turns = jnp.concatenate(
        [
            x if a == 0 else jnp.concatenate([x[:, 128 * a :], x[:, : 128 * a]], axis=1)
            for a in range(8)
        ],
        axis=0,
    )
    x_hi, x_lo = pieces_of(turns, 2)
    k_hi, k_lo = g_hi[...].astype(jnp.bfloat16), g_lo[...].astype(jnp.bfloat16)
    y = dot_t(x_hi, k_hi) + (dot_t(x_lo, k_hi) + dot_t(x_hi, k_lo))
    for a in range(8):
        one, two = y[32 * a : 32 * a + 16], y[32 * a + 16 : 32 * a + 32]
        smooth_out[2 * a] = jnp.where(upper, pltpu.roll(two, 64, 1), one)
        smooth_out[2 * a + 1] = jnp.where(upper, two, pltpu.roll(one, 64, 1))
    for r in range(1, n_az):
        peer = axis_ring(n_az, az, r)
        remote(
            smooth_out.at[peer], smooth_in.at[az], bulk_send.at[3], bulk_recv.at[3], ax, peer
        ).start()
    all_smooth = remote(
        smooth_out.at[most], smooth_in.at[most], bulk_send.at[3], bulk_recv.at[3], ax, right_az
    )
    smooth_in[az] = smooth_out[az]
    @pl.when(ax < n_ax - 1)
    def _():
        halo_down.wait_recv()

    @pl.when(ax > 0)
    def _():
        halo_up.wait_recv()

    def along(p, carry):
        for f in range(5):
            raw[f, p] = raw[f, p] + axial_gain * (
                8.0 * (axial[p + 3, f] - axial[p + 1, f]) - (axial[p + 4, f] - axial[p, f])
            )
        return carry

    lax.fori_loop(0, 8, along, 0)

    all_smooth.wait_recv()
    cycles = lane < 8

    def turn_back(f, carry):
        for a in range(4):
            line = smooth_in[
                pl.ds((a // 2) * 8, 8), pl.ds(f * 2 + a % 2, 1), :
            ].reshape(8, 128)
            tile = jnp.concatenate([line, jnp.zeros((120, 128), jnp.float32)], axis=0).T
            for b in range(2):
                raw[f, 2 * a + b] = jnp.where(
                    cycles, tile[64 * b : 64 * b + 64], raw[f, 2 * a + b]
                )
        return carry

    lax.fori_loop(0, 5, turn_back, 0)
    section_copy = pltpu.make_async_copy(raw, out_ref, load_sem.at[0])
    section_copy.start()
    all_rows.wait_recv()
    total = rows[ax]
    for r in range(1, n_ax):
        total = total + rows_in[r - 1]
    sig_ref[...] = jnp.concatenate([total[:, :64], total[:, 64:]], axis=0)

    section_copy.wait()
    for copy in (edge_low, edge_high, all_sums, all_lines, all_rows, all_smooth):
        copy.wait_send()

    @pl.when(ax > 0)
    def _():
        inner_down.wait_send()
        halo_down.wait_send()

    @pl.when(ax < n_ax - 1)
    def _():
        inner_up.wait_send()
        halo_up.wait_send()


def on_device(conserved, panel_cells, panel_counts, time_bins, amplitudes):
    f32 = jnp.float32
    vmem = pl.BlockSpec(memory_space=pltpu.VMEM)
    smem = pl.BlockSpec(memory_space=pltpu.SMEM)
    hbm = pl.BlockSpec(memory_space=pl.ANY)
    dma = pltpu.SemaphoreType.DMA

    def in_hbm(value):
        return pltpu.with_memory_space_constraint(value, pltpu.HBM)

    section, signal = pl.pallas_call(
        step_kernel,
        out_shape=(
            pltpu.VMEM(conserved.shape, f32),
            jax.ShapeDtypeStruct((2, 64), f32),
        ),
        in_specs=[smem] + [hbm] * 5,
        out_specs=(hbm, vmem),
        scratch_shapes=[
            pltpu.VMEM((5, 8, 64, 128), f32),
            pltpu.VMEM((1, 512), jnp.int32),
            pltpu.VMEM((5, 8, 64, 128), f32),
            pltpu.VMEM((64, 512), jnp.int32),
            pltpu.VMEM((64, 512), f32),
            pltpu.VMEM((8, 1024), f32),
            pltpu.VMEM((12, 5, 64, 128), f32),
            pltpu.VMEM((5, 8, 80, 128), f32),
            pltpu.VMEM((512, 128), f32),
            pltpu.VMEM((2, 5, 2, 8, 128), f32),
            pltpu.VMEM((2, 5, 2, 8, 128), f32),
            pltpu.VMEM((6, 5, 8, 128), f32),
            pltpu.VMEM((16, 16, 128), f32),
            pltpu.VMEM((16, 16, 128), f32),
            pltpu.VMEM((16, 16, 128), f32),
            pltpu.VMEM((16, 16, 128), f32),
            pltpu.VMEM((16, 32, 128), f32),
            pltpu.VMEM((15, 32, 128), f32),
            pltpu.VMEM((32, 1, 128), f32),
            pltpu.VMEM((31, 1, 128), f32),
            pltpu.VMEM((128, 1024), f32),
            pltpu.VMEM((128, 1024), f32),
            dma((4,)),
            dma((8,)),
            dma((6,)),
            dma((6,)),
            dma((4,)),
            dma((4,)),
        ],
        compiler_params=pltpu.CompilerParams(
            collective_id=0, has_side_effects=True, vmem_limit_bytes=24 << 20
        ),
        name="step",
    )(
        panel_counts,
        in_hbm(panel_cells.reshape(1, panel_cells.shape[0])),
        in_hbm(conserved),
        in_hbm(time_bins.T),
        in_hbm(amplitudes.T),
        in_hbm(jnp.asarray(filter_rows())),
    )
    return (section, signal.T)


def solution(mesh):
    placed = (
        P(None, "ax", "az", None),
        P(("ax", "az")),
        P(("ax", "az")),
        P(("ax", "az"), None),
        P(("ax", "az"), None),
    )
    return jax.shard_map(
        on_device,
        mesh=mesh,
        in_specs=placed,
        out_specs=(P(None, "ax", "az", None), P(None, ("ax", "az"))),
        check_vma=False,
    )
```

```python
import math

import jax
import jax.numpy as jnp
import numpy as np
from jax import lax
from jax.experimental import pallas as pl
from jax.experimental.pallas import tpu as pltpu
from jax.sharding import PartitionSpec as P

AZIMUTH = 1024
CYCLES = 8
OBSERVERS = 64
BINS = 1024
MESH = pl.DeviceIdType.MESH

gas_factor = 0.4
time_step = 0.02
ref_pressure = 0.95


def filter_rows():
    n = AZIMUTH
    modes = np.arange(n // 2 + 1, dtype=np.float64)
    lag = np.arange(n)
    factor = np.where((modes == 0) | (modes == n // 2), 1.0, 2.0) / n
    table = np.cos((modes[:, None] * lag[None, :]) % n * (2.0 * np.pi / n))
    rows = np.zeros((CYCLES, 8, n), np.float32)
    for j in range(CYCLES):
        weight = np.exp(-((modes / (4.0 * (j + 1))) ** 8)) * factor
        h = weight @ table
        for r in range(8):
            rows[j, r] = np.roll(h, r)
    return rows


def pieces_of(value, count):
    out = []
    for _ in range(count - 1):
        part = value.astype(jnp.bfloat16)
        out.append(part)
        value = value - part.astype(jnp.float32)
    out.append(value.astype(jnp.bfloat16))
    return out


def dot_t(a, b):
    return lax.dot_general(a, b, (((1,), (1,)), ((), ())), preferred_element_type=jnp.float32)


def axis_ring(n, me, r):
    return lax.rem(me + r, n)


def step_kernel(
    count,
    cells_hbm,
    q_hbm,
    bins_hbm,
    amp_hbm,
    h_hbm,
    out_ref,
    sig_ref,
    raw,
    cells_ref,
    q,
    bins,
    amp,
    h,
    axial,
    relay,
    swirl,
    excess,
    edge_out,
    edge_in,
    inner,
    turned,
    lines_out,
    lines_in,
    smooth_out,
    smooth_in,
    sums,
    sums_in,
    rows,
    rows_in,
    g_hi,
    g_lo,
    load_sem,
    plane_sem,
    near_send,
    near_recv,
    bulk_send,
    bulk_recv,
):
    n_ax, n_az = 32, 16
    ax, az = lax.axis_index("ax"), lax.axis_index("az")

    def remote(source, target, send, recv, ax_to, az_to):
        return pltpu.make_async_remote_copy(
            src_ref=source,
            dst_ref=target,
            send_sem=send,
            recv_sem=recv,
            device_id=(ax_to, az_to),
            device_id_type=MESH,
        )

    loads = [
        pltpu.make_async_copy(cells_hbm, cells_ref, load_sem.at[0]),
        pltpu.make_async_copy(bins_hbm, bins, load_sem.at[1]),
        pltpu.make_async_copy(amp_hbm, amp, load_sem.at[2]),
        pltpu.make_async_copy(h_hbm.at[lax.rem(az, CYCLES)], h, load_sem.at[3]),
    ]

    def plane_load(p):
        return pltpu.make_async_copy(q_hbm.at[:, p], q.at[:, p], plane_sem.at[p])

    for p in range(8):
        plane_load(p).start()
    for copy in loads:
        copy.start()
    barrier = pltpu.get_barrier_semaphore()
    for k in range(1, n_ax):
        r = n_ax // 2 + (k // 2 if k % 2 == 0 else -(k // 2))
        pl.semaphore_signal(
            barrier, inc=1, device_id=(axis_ring(n_ax, ax, r), az), device_id_type=MESH
        )
    for r in range(1, n_az):
        pl.semaphore_signal(
            barrier, inc=1, device_id=(ax, axis_ring(n_az, az, r)), device_id_type=MESH
        )

    lane = lax.broadcasted_iota(jnp.int32, (1, 128), 1)
    radius = lane.astype(jnp.float32) + 0.5
    over_r = 1.0 / radius
    step = jnp.float32(time_step)
    dtheta = 2.0 * math.pi / AZIMUTH
    near = (8.0 / 12.0) * step * over_r
    far = (1.0 / 12.0) * step * over_r
    plus_1 = jnp.where(lane < 127, -near, 0.0)
    minus_1 = jnp.where(lane > 0, near, 0.0)
    plus_2 = jnp.where(lane < 126, far, 0.0)
    minus_2 = jnp.where(lane > 1, -far, 0.0)
    swirl_gain = (-1.0 / 12.0) * step / (radius * dtheta)
    axial_gain = -time_step / 12.0


    def local(p, carry):
        plane_load(p).wait()
        for at in range(0, 64, 16):
            part = pl.ds(at, 16)
            q0, q1, q2, q3, q4 = [q[f, p, part, :] for f in range(5)]
            over = 1.0 / q0
            u, v, w = q1 * over, q2 * over, q3 * over
            pressure = gas_factor * (q4 - 0.5 * (q1 * u + q2 * v + q3 * w))
            excess[pl.ds(pl.multiple_of(p * 64 + at, 16), 16), :] = pressure - ref_pressure
            total = q4 + pressure
            for f, value in enumerate((q1, q1 * u + pressure, q2 * u, q3 * u, total * u)):
                axial[p + 2, f, part, :] = value
            into = pl.ds(at + 8, 16)
            q3w = q3 * w
            for f, value in enumerate((q3, q1 * w, q2 * w, q3w + pressure, total * w)):
                swirl[f, p, into, :] = value
            q3v = q3 * v
            force = step * over_r
            old = (q0, q1, q2 + force * (pressure + q3w), q3 - force * q3v, q4)
            for f, value in enumerate((q2, q1 * v, q2 * v + pressure, q3v, total * v)):
                value = value * radius
                raw[f, p, part, :] = (
                    old[f]
                    + plus_1 * pltpu.roll(value, 127, 1)
                    + minus_1 * pltpu.roll(value, 1, 1)
                    + plus_2 * pltpu.roll(value, 126, 1)
                    + minus_2 * pltpu.roll(value, 2, 1)
                )
        return carry

    lax.fori_loop(0, 8, local, 0)

    for f in range(5):
        for r in range(2):
            edge_out[0, f, r] = swirl[f, :, 8 + r, :]
            edge_out[1, f, r] = swirl[f, :, 70 + r, :]

    def turn_axial(f, carry):
        for a in range(4):
            tile = jnp.concatenate([axial[2 * a + 2, f], axial[2 * a + 3, f]], axis=0)
            inner[a + 1, f] = tile.T[:8]
        return carry

    lax.fori_loop(0, 5, turn_axial, 0)


    @pl.when(ax == 0)
    def _():
        inner[0] = jnp.zeros_like(inner[0])
        axial[0:2] = jnp.zeros((2, 5, 64, 128), jnp.float32)

    @pl.when(ax == n_ax - 1)
    def _():
        inner[5] = jnp.zeros_like(inner[5])
        axial[10:12] = jnp.zeros((2, 5, 64, 128), jnp.float32)

    slots = cells_ref.shape[1]
    loads[0].wait()
    parts = jnp.concatenate(pieces_of(excess[...].T, 3), axis=0)
    cells = cells_ref[...]
    row_hot = lax.broadcasted_iota(jnp.int32, (512, slots), 0) == (cells >> 7)
    row_hot = jnp.where(row_hot, 1.0, 0.0).astype(jnp.bfloat16)
    picked = jnp.dot(parts, row_hot, preferred_element_type=jnp.float32)
    picked = picked[:128] + picked[128:256] + picked[256:]
    lane_hot = lax.broadcasted_iota(jnp.int32, (128, slots), 0) == (cells & 127)
    sampled = jnp.sum(jnp.where(lane_hot, picked, 0.0), axis=0, keepdims=True)
    live = lax.broadcasted_iota(jnp.int32, (1, slots), 1) < count[0]
    sampled = jnp.where(live, sampled, 0.0)
    sixteen = lax.broadcasted_iota(jnp.int32, (16, slots), 0)
    ladder = [(sixteen + 16 * k).astype(jnp.float32).astype(jnp.bfloat16) for k in range(4)]
    one, none = jnp.bfloat16(1.0), jnp.bfloat16(0.0)

    def spread(value, k):
        return jnp.broadcast_to(value[k : k + 1], (16, slots)).astype(jnp.bfloat16)

    loads[1].wait()
    loads[2].wait()

    def group(i, carry):
        ready = []
        for top in range(2):
            at = pl.ds(pl.multiple_of(top * 32 + i * 8, 8), 8)
            b = bins[at, :]
            contrib = sampled * amp[at, :]
            main = contrib.astype(jnp.bfloat16).astype(jnp.float32)
            owner = ((b >> 1) & 15).astype(jnp.float32)
            rest = (((b & 1) << 5) | (b >> 5)).astype(jnp.float32)
            ready.append((main, contrib - main, owner, rest))
        for k in range(8):
            halves = []
            for main, left_over, owner, rest in ready:
                hit = spread(owner, k) == ladder[0]
                left = jnp.concatenate(
                    [jnp.where(hit, spread(part, k), none) for part in (main, left_over)], axis=0
                )
                place = spread(rest, k)
                right = jnp.concatenate(
                    [jnp.where(place == rung, one, none) for rung in ladder], axis=0
                )
                both = dot_t(left, right)
                halves.append(both[:16] + both[16:])
            sums[:, pl.ds(i * 8 + k, 1), :] = jnp.concatenate(halves, axis=1).reshape(16, 1, 128)
        return carry

    lax.fori_loop(0, 4, group, 0)

    pl.semaphore_wait(barrier, n_ax - 1 + n_az - 1)
    below, above = axis_ring(n_ax, ax, n_ax - 1), axis_ring(n_ax, ax, 1)
    left_az, right_az = axis_ring(n_az, az, n_az - 1), axis_ring(n_az, az, 1)
    edge_low = remote(
        edge_out.at[0], edge_in.at[1], near_send.at[0], near_recv.at[0], ax, left_az
    )
    edge_high = remote(
        edge_out.at[1], edge_in.at[0], near_send.at[1], near_recv.at[1], ax, right_az
    )
    inner_down = remote(inner.at[1], inner.at[5], near_send.at[2], near_recv.at[2], below, az)
    inner_up = remote(inner.at[4], inner.at[0], near_send.at[3], near_recv.at[3], above, az)
    halo_down = remote(
        axial.at[pl.ds(2, 2)],
        axial.at[pl.ds(10, 2)],
        near_send.at[4],
        near_recv.at[4],
        below,
        az,
    )
    halo_up = remote(
        axial.at[pl.ds(8, 2)],
        axial.at[pl.ds(0, 2)],
        near_send.at[5],
        near_recv.at[5],
        above,
        az,
    )
    @pl.when(ax > 0)
    def _():
        inner_down.start()

    @pl.when(ax < n_ax - 1)
    def _():
        inner_up.start()

    edge_low.start()
    edge_high.start()

    @pl.when(jnp.logical_and(ax > 0, ax != n_ax // 2))
    def _():
        halo_down.start()

    @pl.when(jnp.logical_and(ax < n_ax - 1, ax != n_ax // 2 - 1))
    def _():
        halo_up.start()

    for r in range(1, n_az):
        peer = axis_ring(n_az, az, r)
        remote(sums.at[peer], sums_in.at[r - 1], bulk_send.at[0], bulk_recv.at[0], ax, peer).start()
    all_sums = remote(
        sums.at[pl.ds(0, 15)], sums_in, bulk_send.at[0], bulk_recv.at[0], ax, right_az
    )

    loads[3].wait()
    first = h[...]
    for k in range(0, 128, 16):
        g = jnp.concatenate(
            [first if k == 0 else pltpu.roll(first, k, 1), pltpu.roll(first, k + 8, 1)], axis=0
        )
        g_hi[k : k + 16], g_lo[k : k + 16] = pieces_of(g, 2)

    for d in range(n_az):
        lines_out[d, 16:24, :] = jnp.zeros((8, 128), jnp.float32)

    def turn_lines(f, carry):
        for a in range(4):
            tile = jnp.concatenate([raw[f, 2 * a], raw[f, 2 * a + 1]], axis=0)
            turned[f, a] = tile.T[:8]
            tile = jnp.concatenate([swirl[f, 2 * a, 8:72, :], swirl[f, 2 * a + 1, 8:72, :]], axis=0)
            lines_out[
                pl.ds((a // 2) * 8, 8), pl.ds(10 + f * 2 + a % 2, 1), :
            ] = tile.T[:8].reshape(8, 1, 128)
        return carry

    lax.fori_loop(0, 5, turn_lines, 0)
    @pl.when(ax < n_ax - 1)
    def _():
        inner_down.wait_recv()

    @pl.when(ax > 0)
    def _():
        inner_up.wait_recv()

    upper = lane >= 64
    for f in range(5):
        for a in range(4):
            before, now, after = inner[a, f], inner[a + 1, f], inner[a + 2, f]
            next_1 = pltpu.roll(jnp.where(upper, now, after), 64, 1)
            last_1 = pltpu.roll(jnp.where(upper, before, now), 64, 1)
            line = turned[f, a] + axial_gain * (8.0 * (next_1 - last_1) - (after - before))
            at = (a // 2) * 8
            row = f * 2 + a % 2
            lines_out[at : at + 8, row : row + 1, :] = line.reshape(8, 1, 128)
    for r in range(1, n_az):
        peer = axis_ring(n_az, az, r)
        remote(
            lines_out.at[peer], lines_in.at[az], bulk_send.at[1], bulk_recv.at[1], ax, peer
        ).start()
    most = pl.ds(0, 15)
    all_lines = remote(
        lines_out.at[most], lines_in.at[most], bulk_send.at[1], bulk_recv.at[1], ax, right_az
    )

    lines_in[az] = lines_out[az]
    middle = n_ax // 2
    quarters = [pl.ds(16 * k, 16) for k in range(4)]
    pair_up, pair_down = pl.ds(8, 2), pl.ds(2, 2)
    land_up, land_down = pl.ds(0, 2), pl.ds(10, 2)
    routes = []
    for k, (by_up, by_down) in enumerate(((n_ax - 1, 0), (middle + 1, middle - 2), (n_ax - 2, 1))):
        rows_k = quarters[k + 1]
        for source, land, start_ax, by, end_ax, lane_of in (
            (pair_up, land_up, middle - 1, by_up, middle, 5),
            (pair_down, land_down, middle, by_down, middle - 1, 4),
        ):
            leg = remote(
                axial.at[source, :, rows_k, :],
                relay,
                near_send.at[lane_of],
                near_recv.at[6],
                by,
                az,
            )
            forward = remote(
                relay,
                axial.at[land, :, rows_k, :],
                near_send.at[6],
                near_recv.at[lane_of],
                end_ax,
                az,
            )
            routes.append((start_ax, by, leg, forward))
    up_direct = remote(
        axial.at[pair_up, :, quarters[0], :],
        axial.at[land_up, :, quarters[0], :],
        near_send.at[5],
        near_recv.at[5],
        middle,
        az,
    )
    down_direct = remote(
        axial.at[pair_down, :, quarters[0], :],
        axial.at[land_down, :, quarters[0], :],
        near_send.at[4],
        near_recv.at[4],
        middle - 1,
        az,
    )
    for begins, _, leg, _ in routes:

        @pl.when(ax == begins)
        def _():
            leg.start()

    edge_low.wait_recv()
    edge_high.wait_recv()
    for f in range(5):
        for r in range(2):
            swirl[f, :, 6 + r, :] = edge_in[0, f, r]
            swirl[f, :, 72 + r, :] = edge_in[1, f, r]

    def around(p, carry):
        for f in range(5):
            raw[f, p] = raw[f, p] + swirl_gain * (
                8.0 * (swirl[f, p, 9:73, :] - swirl[f, p, 7:71, :])
                - (swirl[f, p, 10:74, :] - swirl[f, p, 6:70, :])
            )
        return carry

    lax.fori_loop(0, 8, around, 0)

    all_sums.wait_recv()
    total = sums[az]
    for r in range(1, n_az):
        total = total + sums_in[r - 1]
    flipped = total.T
    rows[...] = jnp.concatenate(
        [flipped[(top * 2 + e) * 32 : (top * 2 + e) * 32 + 32] for e in range(2) for top in range(2)],
        axis=1,
    ).reshape(n_ax, 1, 128)
    for r in range(1, n_ax):
        peer = axis_ring(n_ax, ax, r)
        remote(rows.at[peer], rows_in.at[r - 1], bulk_send.at[2], bulk_recv.at[2], peer, az).start()
    all_rows = remote(
        rows.at[pl.ds(0, 31)], rows_in, bulk_send.at[2], bulk_recv.at[2], above, az
    )

    for begins, direct in ((middle - 1, up_direct), (middle, down_direct)):

        @pl.when(ax == begins)
        def _():
            direct.start()

    all_lines.wait_recv()

    def relay_on(some):
        for _, by, leg, forward in some:

            @pl.when(ax == by)
            def _():
                leg.wait_recv()
                forward.start()

    relay_on(routes[:2])
    low, high = [], []
    for s in range(0, n_az, 2):
        one, two = lines_in[s], lines_in[s + 1]
        low.append(jnp.where(upper, pltpu.roll(two, 64, 1), one))
        high.append(jnp.where(upper, two, pltpu.roll(one, 64, 1)))
    cycle = lax.rem(az, CYCLES).astype(jnp.float32) + 0.5
    gain = jnp.full((1, 128), -time_step / 12.0 / dtheta, jnp.float32) / cycle
    gain = gain[:, :1]

    def completed(both):
        change = 8.0 * (
            pltpu.roll(both, AZIMUTH - 1, 1) - pltpu.roll(both, 1, 1)
        ) - (pltpu.roll(both, AZIMUTH - 2, 1) - pltpu.roll(both, 2, 1))
        return both[:16] + gain * pltpu.roll(change, 14, 0)[:16]

    x = jnp.concatenate(
        [completed(jnp.concatenate(low, axis=1)), completed(jnp.concatenate(high, axis=1))], axis=0
    )

    def turns(part):
        return jnp.concatenate(
            [
                part
                if a == 0
                else jnp.concatenate([part[:, 128 * a :], part[:, : 128 * a]], axis=1)
                for a in range(8)
            ],
            axis=0,
        )

    x_hi, x_lo = [turns(part) for part in pieces_of(x, 2)]
    k_hi, k_lo = g_hi[...], g_lo[...]
    y = dot_t(x_hi, k_hi) + (dot_t(x_lo, k_hi) + dot_t(x_hi, k_lo))
    for a in range(8):
        one, two = y[32 * a : 32 * a + 16], y[32 * a + 16 : 32 * a + 32]
        smooth_out[2 * a] = jnp.where(upper, pltpu.roll(two, 64, 1), one)
        smooth_out[2 * a + 1] = jnp.where(upper, two, pltpu.roll(one, 64, 1))
    for r in range(1, n_az):
        peer = axis_ring(n_az, az, r)
        remote(
            smooth_out.at[peer], smooth_in.at[az], bulk_send.at[3], bulk_recv.at[3], ax, peer
        ).start()
    all_smooth = remote(
        smooth_out.at[most], smooth_in.at[most], bulk_send.at[3], bulk_recv.at[3], ax, right_az
    )
    smooth_in[az] = smooth_out[az]
    relay_on(routes[2:])
    @pl.when(ax < n_ax - 1)
    def _():
        halo_down.wait_recv()

    @pl.when(ax > 0)
    def _():
        halo_up.wait_recv()

    def along(p, carry):
        for f in range(5):
            raw[f, p] = raw[f, p] + axial_gain * (
                8.0 * (axial[p + 3, f] - axial[p + 1, f]) - (axial[p + 4, f] - axial[p, f])
            )
        return carry

    lax.fori_loop(0, 8, along, 0)

    all_smooth.wait_recv()
    cycles = lane < 8

    def turn_back(f, carry):
        for a in range(4):
            line = smooth_in[
                pl.ds((a // 2) * 8, 8), pl.ds(f * 2 + a % 2, 1), :
            ].reshape(8, 128)
            tile = jnp.concatenate([line, jnp.zeros((120, 128), jnp.float32)], axis=0).T
            for b in range(2):
                raw[f, 2 * a + b] = jnp.where(
                    cycles, tile[64 * b : 64 * b + 64], raw[f, 2 * a + b]
                )
        return carry

    lax.fori_loop(0, 5, turn_back, 0)
    section_copy = pltpu.make_async_copy(raw, out_ref, load_sem.at[0])
    section_copy.start()
    all_rows.wait_recv()
    total = rows[ax]
    for r in range(1, n_ax):
        total = total + rows_in[r - 1]
    sig_ref[...] = jnp.concatenate([total[:, :64], total[:, 64:]], axis=0)

    section_copy.wait()
    for copy in (edge_low, edge_high, all_sums, all_lines, all_rows, all_smooth):
        copy.wait_send()

    @pl.when(ax > 0)
    def _():
        inner_down.wait_send()
        halo_down.wait_send()

    @pl.when(ax < n_ax - 1)
    def _():
        inner_up.wait_send()
        halo_up.wait_send()

    for _, by, _, forward in routes:

        @pl.when(ax == by)
        def _():
            forward.wait_send()


def leave_kernel(raw, sig, section_ref, sig_ref, sem):
    copies = [
        pltpu.make_async_copy(raw.at[f], section_ref.at[f], sem.at[f]) for f in range(5)
    ] + [pltpu.make_async_copy(sig, sig_ref, sem.at[5])]
    for copy in copies:
        copy.start()
    for copy in copies:
        copy.wait()


def on_device(conserved, panel_cells, panel_counts, time_bins, amplitudes):
    f32 = jnp.float32
    vmem = pl.BlockSpec(memory_space=pltpu.VMEM)
    smem = pl.BlockSpec(memory_space=pltpu.SMEM)
    hbm = pl.BlockSpec(memory_space=pl.ANY)
    dma = pltpu.SemaphoreType.DMA

    def in_hbm(value):
        return pltpu.with_memory_space_constraint(value, pltpu.HBM)

    def in_vmem(value):
        return pltpu.with_memory_space_constraint(value, pltpu.VMEM)

    section, signal = pl.pallas_call(
        step_kernel,
        out_shape=(
            pltpu.VMEM(conserved.shape, f32),
            pltpu.VMEM((2, 64), f32),
        ),
        in_specs=[smem] + [hbm] * 5,
        out_specs=(hbm, vmem),
        scratch_shapes=[
            pltpu.VMEM((5, 8, 64, 128), f32),
            pltpu.VMEM((1, 512), jnp.int32),
            pltpu.VMEM((5, 8, 64, 128), f32),
            pltpu.VMEM((64, 512), jnp.int32),
            pltpu.VMEM((64, 512), f32),
            pltpu.VMEM((8, 1024), f32),
            pltpu.VMEM((12, 5, 64, 128), f32),
            pltpu.VMEM((2, 5, 16, 128), f32),
            pltpu.VMEM((5, 8, 80, 128), f32),
            pltpu.VMEM((512, 128), f32),
            pltpu.VMEM((2, 5, 2, 8, 128), f32),
            pltpu.VMEM((2, 5, 2, 8, 128), f32),
            pltpu.VMEM((6, 5, 8, 128), f32),
            pltpu.VMEM((5, 4, 8, 128), f32),
            pltpu.VMEM((16, 24, 128), f32),
            pltpu.VMEM((16, 24, 128), f32),
            pltpu.VMEM((16, 16, 128), f32),
            pltpu.VMEM((16, 16, 128), f32),
            pltpu.VMEM((16, 32, 128), f32),
            pltpu.VMEM((15, 32, 128), f32),
            pltpu.VMEM((32, 1, 128), f32),
            pltpu.VMEM((31, 1, 128), f32),
            pltpu.VMEM((128, 1024), jnp.bfloat16),
            pltpu.VMEM((128, 1024), jnp.bfloat16),
            dma((4,)),
            dma((8,)),
            dma((7,)),
            dma((7,)),
            dma((4,)),
            dma((4,)),
        ],
        compiler_params=pltpu.CompilerParams(
            collective_id=0, has_side_effects=True, vmem_limit_bytes=24 << 20
        ),
        name="step",
    )(
        panel_counts,
        in_hbm(panel_cells.reshape(1, panel_cells.shape[0])),
        in_hbm(conserved),
        in_hbm(time_bins.T),
        in_hbm(amplitudes.T),
        in_hbm(jnp.asarray(filter_rows())),
    )
    section, signal = pl.pallas_call(
        leave_kernel,
        out_shape=(
            jax.ShapeDtypeStruct(conserved.shape, f32),
            jax.ShapeDtypeStruct((2, 64), f32),
        ),
        in_specs=[hbm, hbm],
        out_specs=(hbm, hbm),
        scratch_shapes=[dma((6,))],
        compiler_params=pltpu.CompilerParams(vmem_limit_bytes=8 << 20),
        name="leave",
    )(in_vmem(section), in_vmem(signal))
    return (section, signal.T)


def solution(mesh):
    placed = (
        P(None, "ax", "az", None),
        P(("ax", "az")),
        P(("ax", "az")),
        P(("ax", "az"), None),
        P(("ax", "az"), None),
    )
    return jax.shard_map(
        on_device,
        mesh=mesh,
        in_specs=placed,
        out_specs=(P(None, "ax", "az", None), P(None, ("ax", "az"))),
        check_vma=False,
    )
```

```python
import math

import jax
import jax.numpy as jnp
import numpy as np
from jax import lax
from jax.experimental import pallas as pl
from jax.experimental.pallas import tpu as pltpu
from jax.sharding import PartitionSpec as P

AZIMUTH = 1024
CYCLES = 8
OBSERVERS = 64
BINS = 1024
MESH = pl.DeviceIdType.MESH

gas_factor = 0.4
time_step = 0.02
ref_pressure = 0.95


def filter_rows():
    n = AZIMUTH
    modes = np.arange(n // 2 + 1, dtype=np.float64)
    lag = np.arange(n)
    factor = np.where((modes == 0) | (modes == n // 2), 1.0, 2.0) / n
    table = np.cos((modes[:, None] * lag[None, :]) % n * (2.0 * np.pi / n))
    rows = np.zeros((CYCLES, 8, n), np.float32)
    for j in range(CYCLES):
        weight = np.exp(-((modes / (4.0 * (j + 1))) ** 8)) * factor
        h = weight @ table
        for r in range(8):
            rows[j, r] = np.roll(h, r)
    return rows


def pieces_of(value, count):
    out = []
    for _ in range(count - 1):
        part = value.astype(jnp.bfloat16)
        out.append(part)
        value = value - part.astype(jnp.float32)
    out.append(value.astype(jnp.bfloat16))
    return out


def dot_t(a, b):
    return lax.dot_general(a, b, (((1,), (1,)), ((), ())), preferred_element_type=jnp.float32)


def axis_ring(n, me, r):
    return lax.rem(me + r, n)


def step_kernel(
    count,
    cells_hbm,
    q_hbm,
    bins_hbm,
    amp_hbm,
    h_hbm,
    out_ref,
    sig_ref,
    raw,
    cells_ref,
    q,
    bins,
    amp,
    h,
    axial,
    relay,
    swirl,
    excess,
    edge_out,
    edge_in,
    inner,
    turned,
    lines_out,
    lines_in,
    smooth_out,
    smooth_in,
    sums,
    sums_in,
    rows,
    rows_in,
    g_hi,
    g_lo,
    load_sem,
    plane_sem,
    near_send,
    near_recv,
    bulk_send,
    bulk_recv,
):
    n_ax, n_az = 32, 16
    ax, az = lax.axis_index("ax"), lax.axis_index("az")

    def remote(source, target, send, recv, ax_to, az_to):
        return pltpu.make_async_remote_copy(
            src_ref=source,
            dst_ref=target,
            send_sem=send,
            recv_sem=recv,
            device_id=(ax_to, az_to),
            device_id_type=MESH,
        )

    loads = [
        pltpu.make_async_copy(cells_hbm, cells_ref, load_sem.at[0]),
        pltpu.make_async_copy(bins_hbm, bins, load_sem.at[1]),
        pltpu.make_async_copy(amp_hbm, amp, load_sem.at[2]),
        pltpu.make_async_copy(h_hbm.at[lax.rem(az, CYCLES)], h, load_sem.at[3]),
    ]

    def plane_load(p):
        return pltpu.make_async_copy(q_hbm.at[:, p], q.at[:, p], plane_sem.at[p])

    for p in range(8):
        plane_load(p).start()
    for copy in loads:
        copy.start()
    for d in range(n_az):
        lines_in[d, 16:24, :] = jnp.zeros((8, 128), jnp.float32)
    barrier = pltpu.get_barrier_semaphore()
    for k in range(1, n_ax):
        r = n_ax // 2 + (k // 2 if k % 2 == 0 else -(k // 2))
        pl.semaphore_signal(
            barrier, inc=1, device_id=(axis_ring(n_ax, ax, r), az), device_id_type=MESH
        )
    for r in range(1, n_az):
        pl.semaphore_signal(
            barrier, inc=1, device_id=(ax, axis_ring(n_az, az, r)), device_id_type=MESH
        )

    lane = lax.broadcasted_iota(jnp.int32, (1, 128), 1)
    radius = lane.astype(jnp.float32) + 0.5
    over_r = 1.0 / radius
    step = jnp.float32(time_step)
    dtheta = 2.0 * math.pi / AZIMUTH
    near = (8.0 / 12.0) * step * over_r
    far = (1.0 / 12.0) * step * over_r
    plus_1 = jnp.where(lane < 127, -near, 0.0)
    minus_1 = jnp.where(lane > 0, near, 0.0)
    plus_2 = jnp.where(lane < 126, far, 0.0)
    minus_2 = jnp.where(lane > 1, -far, 0.0)
    swirl_gain = (-1.0 / 12.0) * step / (radius * dtheta)
    axial_gain = -time_step / 12.0


    def local(p, carry):
        plane_load(p).wait()
        for at in range(0, 64, 16):
            part = pl.ds(at, 16)
            q0, q1, q2, q3, q4 = [q[f, p, part, :] for f in range(5)]
            over = 1.0 / q0
            u, v, w = q1 * over, q2 * over, q3 * over
            pressure = gas_factor * (q4 - 0.5 * (q1 * u + q2 * v + q3 * w))
            excess[pl.ds(pl.multiple_of(p * 64 + at, 16), 16), :] = pressure - ref_pressure
            total = q4 + pressure
            for f, value in enumerate((q1, q1 * u + pressure, q2 * u, q3 * u, total * u)):
                axial[p + 2, f, part, :] = value
            into = pl.ds(at + 8, 16)
            q3w = q3 * w
            for f, value in enumerate((q3, q1 * w, q2 * w, q3w + pressure, total * w)):
                swirl[f, p, into, :] = value
            q3v = q3 * v
            force = step * over_r
            old = (q0, q1, q2 + force * (pressure + q3w), q3 - force * q3v, q4)
            for f, value in enumerate((q2, q1 * v, q2 * v + pressure, q3v, total * v)):
                value = value * radius
                raw[f, p, part, :] = (
                    old[f]
                    + plus_1 * pltpu.roll(value, 127, 1)
                    + minus_1 * pltpu.roll(value, 1, 1)
                    + plus_2 * pltpu.roll(value, 126, 1)
                    + minus_2 * pltpu.roll(value, 2, 1)
                )
        return carry

    lax.fori_loop(0, 8, local, 0)

    for f in range(5):
        for r in range(2):
            edge_out[0, f, r] = swirl[f, :, 8 + r, :]
            edge_out[1, f, r] = swirl[f, :, 70 + r, :]

    def turn_axial(f, carry):
        for a in range(4):
            tile = jnp.concatenate([axial[2 * a + 2, f], axial[2 * a + 3, f]], axis=0)
            inner[a + 1, f] = tile.T[:8]
        return carry

    lax.fori_loop(0, 5, turn_axial, 0)


    @pl.when(ax == 0)
    def _():
        inner[0] = jnp.zeros_like(inner[0])
        axial[0:2] = jnp.zeros((2, 5, 64, 128), jnp.float32)

    @pl.when(ax == n_ax - 1)
    def _():
        inner[5] = jnp.zeros_like(inner[5])
        axial[10:12] = jnp.zeros((2, 5, 64, 128), jnp.float32)

    slots = cells_ref.shape[1]
    loads[0].wait()
    parts = jnp.concatenate(pieces_of(excess[...].T, 3), axis=0)
    cells = cells_ref[...]
    row_hot = lax.broadcasted_iota(jnp.int32, (512, slots), 0) == (cells >> 7)
    row_hot = jnp.where(row_hot, 1.0, 0.0).astype(jnp.bfloat16)
    picked = jnp.dot(parts, row_hot, preferred_element_type=jnp.float32)
    picked = picked[:128] + picked[128:256] + picked[256:]
    lane_hot = lax.broadcasted_iota(jnp.int32, (128, slots), 0) == (cells & 127)
    sampled = jnp.sum(jnp.where(lane_hot, picked, 0.0), axis=0, keepdims=True)
    live = lax.broadcasted_iota(jnp.int32, (1, slots), 1) < count[0]
    sampled = jnp.where(live, sampled, 0.0)
    sixteen = lax.broadcasted_iota(jnp.int32, (16, slots), 0)
    ladder = [(sixteen + 16 * k).astype(jnp.float32).astype(jnp.bfloat16) for k in range(4)]
    one, none = jnp.bfloat16(1.0), jnp.bfloat16(0.0)

    def spread(value, k):
        return jnp.broadcast_to(value[k : k + 1], (16, slots)).astype(jnp.bfloat16)

    loads[1].wait()
    loads[2].wait()

    def group(i, carry):
        ready = []
        for top in range(2):
            at = pl.ds(pl.multiple_of(top * 32 + i * 8, 8), 8)
            b = bins[at, :]
            contrib = sampled * amp[at, :]
            main = contrib.astype(jnp.bfloat16).astype(jnp.float32)
            owner = ((b >> 1) & 15).astype(jnp.float32)
            rest = (((b & 1) << 5) | (b >> 5)).astype(jnp.float32)
            ready.append((main, contrib - main, owner, rest))
        for k in range(8):
            halves = []
            for main, left_over, owner, rest in ready:
                hit = spread(owner, k) == ladder[0]
                left = jnp.concatenate(
                    [jnp.where(hit, spread(part, k), none) for part in (main, left_over)], axis=0
                )
                place = spread(rest, k)
                right = jnp.concatenate(
                    [jnp.where(place == rung, one, none) for rung in ladder], axis=0
                )
                both = dot_t(left, right)
                halves.append(both[:16] + both[16:])
            sums[:, pl.ds(i * 8 + k, 1), :] = jnp.concatenate(halves, axis=1).reshape(16, 1, 128)
        return carry

    lax.fori_loop(0, 4, group, 0)

    pl.semaphore_wait(barrier, n_ax - 1 + n_az - 1)
    below, above = axis_ring(n_ax, ax, n_ax - 1), axis_ring(n_ax, ax, 1)
    left_az, right_az = axis_ring(n_az, az, n_az - 1), axis_ring(n_az, az, 1)
    edge_low = remote(
        edge_out.at[0], edge_in.at[1], near_send.at[0], near_recv.at[0], ax, left_az
    )
    edge_high = remote(
        edge_out.at[1], edge_in.at[0], near_send.at[1], near_recv.at[1], ax, right_az
    )
    inner_down = remote(inner.at[1], inner.at[5], near_send.at[2], near_recv.at[2], below, az)
    inner_up = remote(inner.at[4], inner.at[0], near_send.at[3], near_recv.at[3], above, az)
    halo_down = remote(
        axial.at[pl.ds(2, 2)],
        axial.at[pl.ds(10, 2)],
        near_send.at[4],
        near_recv.at[4],
        below,
        az,
    )
    halo_up = remote(
        axial.at[pl.ds(8, 2)],
        axial.at[pl.ds(0, 2)],
        near_send.at[5],
        near_recv.at[5],
        above,
        az,
    )
    @pl.when(ax > 0)
    def _():
        inner_down.start()

    @pl.when(ax < n_ax - 1)
    def _():
        inner_up.start()

    edge_low.start()
    edge_high.start()

    @pl.when(jnp.logical_and(ax > 0, ax != n_ax // 2))
    def _():
        halo_down.start()

    @pl.when(jnp.logical_and(ax < n_ax - 1, ax != n_ax // 2 - 1))
    def _():
        halo_up.start()

    for r in range(1, n_az):
        peer = axis_ring(n_az, az, r)
        remote(sums.at[peer], sums_in.at[r - 1], bulk_send.at[0], bulk_recv.at[0], ax, peer).start()
    all_sums = remote(
        sums.at[pl.ds(0, 15)], sums_in, bulk_send.at[0], bulk_recv.at[0], ax, right_az
    )

    loads[3].wait()
    first = h[...]
    for k in range(0, 128, 16):
        g = jnp.concatenate(
            [first if k == 0 else pltpu.roll(first, k, 1), pltpu.roll(first, k + 8, 1)], axis=0
        )
        g_hi[k : k + 16], g_lo[k : k + 16] = pieces_of(g, 2)

    for d in range(n_az):
        lines_out[d, 16:24, :] = jnp.zeros((8, 128), jnp.float32)

    def turn_lines(f, carry):
        for a in range(4):
            tile = jnp.concatenate([raw[f, 2 * a], raw[f, 2 * a + 1]], axis=0)
            turned[f, a] = tile.T[:8]
            tile = jnp.concatenate([swirl[f, 2 * a, 8:72, :], swirl[f, 2 * a + 1, 8:72, :]], axis=0)
            lines_out[
                pl.ds((a // 2) * 8, 8), pl.ds(10 + f * 2 + a % 2, 1), :
            ] = tile.T[:8].reshape(8, 1, 128)
        return carry

    lax.fori_loop(0, 5, turn_lines, 0)
    @pl.when(ax < n_ax - 1)
    def _():
        inner_down.wait_recv()

    @pl.when(ax > 0)
    def _():
        inner_up.wait_recv()

    upper = lane >= 64
    for f in range(5):
        for a in range(4):
            before, now, after = inner[a, f], inner[a + 1, f], inner[a + 2, f]
            next_1 = pltpu.roll(jnp.where(upper, now, after), 64, 1)
            last_1 = pltpu.roll(jnp.where(upper, before, now), 64, 1)
            line = turned[f, a] + axial_gain * (8.0 * (next_1 - last_1) - (after - before))
            at = (a // 2) * 8
            row = f * 2 + a % 2
            lines_out[at : at + 8, row : row + 1, :] = line.reshape(8, 1, 128)
    filled = pl.ds(0, 20)
    for r in range(1, n_az):
        peer = axis_ring(n_az, az, r)
        remote(
            lines_out.at[peer, filled], lines_in.at[az, filled], bulk_send.at[1], bulk_recv.at[1], ax, peer
        ).start()
    most = pl.ds(0, 15)
    all_lines = remote(
        lines_out.at[most, filled], lines_in.at[most, filled], bulk_send.at[1], bulk_recv.at[1], ax, right_az
    )

    lines_in[az] = lines_out[az]
    middle = n_ax // 2
    pair_up, land_up = pl.ds(8, 2), pl.ds(0, 2)
    routes = []
    for by, start, size, place, slot in (
        (n_ax - 1, 8, 24, 0, 6),
        (n_ax - 1, 32, 16, 24, 7),
        (middle + 1, 48, 8, 0, 6),
        (n_ax - 2, 56, 8, 0, 6),
    ):
        share = pl.ds(start, size)
        stop = relay.at[:, :, pl.ds(place, size), :]
        leg = remote(
            axial.at[pair_up, :, share, :], stop, near_send.at[5], near_recv.at[slot], by, az
        )
        forward = remote(
            stop, axial.at[land_up, :, share, :], near_send.at[slot], near_recv.at[5], middle, az
        )
        routes.append((middle - 1, by, leg, forward))
    share = pl.ds(0, 8)
    up_direct = remote(
        axial.at[pair_up, :, share, :],
        axial.at[land_up, :, share, :],
        near_send.at[5],
        near_recv.at[5],
        middle,
        az,
    )
    for begins, _, leg, _ in routes:

        @pl.when(ax == begins)
        def _():
            leg.start()

    edge_low.wait_recv()
    edge_high.wait_recv()
    for f in range(5):
        for r in range(2):
            swirl[f, :, 6 + r, :] = edge_in[0, f, r]
            swirl[f, :, 72 + r, :] = edge_in[1, f, r]

    def around(p, carry):
        for f in range(5):
            raw[f, p] = raw[f, p] + swirl_gain * (
                8.0 * (swirl[f, p, 9:73, :] - swirl[f, p, 7:71, :])
                - (swirl[f, p, 10:74, :] - swirl[f, p, 6:70, :])
            )
        return carry

    lax.fori_loop(0, 8, around, 0)

    all_sums.wait_recv()
    total = sums[az]
    for r in range(1, n_az):
        total = total + sums_in[r - 1]
    flipped = total.T
    rows[...] = jnp.concatenate(
        [flipped[(top * 2 + e) * 32 : (top * 2 + e) * 32 + 32] for e in range(2) for top in range(2)],
        axis=1,
    ).reshape(n_ax, 1, 128)
    for r in range(1, n_ax):
        peer = axis_ring(n_ax, ax, r)
        remote(rows.at[peer], rows_in.at[r - 1], bulk_send.at[2], bulk_recv.at[2], peer, az).start()
    all_rows = remote(
        rows.at[pl.ds(0, 31)], rows_in, bulk_send.at[2], bulk_recv.at[2], above, az
    )

    @pl.when(ax == middle - 1)
    def _():
        up_direct.start()

    @pl.when(ax == middle)
    def _():
        halo_down.start()

    def relay_on(some):
        for _, by, leg, forward in some:

            @pl.when(ax == by)
            def _():
                leg.wait_recv()
                forward.start()

    relay_on(routes[:1])
    all_lines.wait_recv()
    relay_on(routes[1:2])

    low, high = [], []
    for s in range(0, n_az, 2):
        one, two = lines_in[s], lines_in[s + 1]
        low.append(jnp.where(upper, pltpu.roll(two, 64, 1), one))
        high.append(jnp.where(upper, two, pltpu.roll(one, 64, 1)))
    cycle = lax.rem(az, CYCLES).astype(jnp.float32) + 0.5
    gain = jnp.full((1, 128), -time_step / 12.0 / dtheta, jnp.float32) / cycle
    gain = gain[:, :1]

    def completed(both):
        change = 8.0 * (
            pltpu.roll(both, AZIMUTH - 1, 1) - pltpu.roll(both, 1, 1)
        ) - (pltpu.roll(both, AZIMUTH - 2, 1) - pltpu.roll(both, 2, 1))
        return both[:16] + gain * pltpu.roll(change, 14, 0)[:16]

    x = jnp.concatenate(
        [completed(jnp.concatenate(low, axis=1)), completed(jnp.concatenate(high, axis=1))], axis=0
    )

    def turns(part):
        return jnp.concatenate(
            [
                part
                if a == 0
                else jnp.concatenate([part[:, 128 * a :], part[:, : 128 * a]], axis=1)
                for a in range(8)
            ],
            axis=0,
        )

    x_hi, x_lo = [turns(part) for part in pieces_of(x, 2)]
    k_hi, k_lo = g_hi[...], g_lo[...]
    y = dot_t(x_hi, k_hi) + (dot_t(x_lo, k_hi) + dot_t(x_hi, k_lo))
    for a in range(8):
        one, two = y[32 * a : 32 * a + 16], y[32 * a + 16 : 32 * a + 32]
        smooth_out[2 * a] = jnp.where(upper, pltpu.roll(two, 64, 1), one)
        smooth_out[2 * a + 1] = jnp.where(upper, two, pltpu.roll(one, 64, 1))
    used = pl.ds(0, 10)
    for r in range(1, n_az):
        peer = axis_ring(n_az, az, r)
        remote(
            smooth_out.at[peer, used], smooth_in.at[az, used], bulk_send.at[3], bulk_recv.at[3], ax, peer
        ).start()
    all_smooth = remote(
        smooth_out.at[most, used], smooth_in.at[most, used], bulk_send.at[3], bulk_recv.at[3], ax, right_az
    )
    smooth_in[az] = smooth_out[az]
    relay_on(routes[2:])
    @pl.when(ax < n_ax - 1)
    def _():
        halo_down.wait_recv()

    @pl.when(ax > 0)
    def _():
        halo_up.wait_recv()

    def along(p, carry):
        for f in range(5):
            raw[f, p] = raw[f, p] + axial_gain * (
                8.0 * (axial[p + 3, f] - axial[p + 1, f]) - (axial[p + 4, f] - axial[p, f])
            )
        return carry

    lax.fori_loop(0, 8, along, 0)

    all_smooth.wait_recv()
    cycles = lane < 8

    def turn_back(f, carry):
        for a in range(4):
            line = smooth_in[
                pl.ds((a // 2) * 8, 8), pl.ds(f * 2 + a % 2, 1), :
            ].reshape(8, 128)
            tile = jnp.concatenate([line, jnp.zeros((120, 128), jnp.float32)], axis=0).T
            for b in range(2):
                raw[f, 2 * a + b] = jnp.where(
                    cycles, tile[64 * b : 64 * b + 64], raw[f, 2 * a + b]
                )
        return carry

    lax.fori_loop(0, 5, turn_back, 0)
    section_copy = pltpu.make_async_copy(raw, out_ref, load_sem.at[0])
    section_copy.start()
    all_rows.wait_recv()
    total = rows[ax]
    for r in range(1, n_ax):
        total = total + rows_in[r - 1]
    sig_ref[...] = jnp.concatenate([total[:, :64], total[:, 64:]], axis=0)

    section_copy.wait()
    for copy in (edge_low, edge_high, all_sums, all_lines, all_rows, all_smooth):
        copy.wait_send()

    @pl.when(ax > 0)
    def _():
        inner_down.wait_send()
        halo_down.wait_send()

    @pl.when(ax < n_ax - 1)
    def _():
        inner_up.wait_send()
        halo_up.wait_send()

    for _, by, _, forward in routes:

        @pl.when(ax == by)
        def _():
            forward.wait_send()


def leave_kernel(raw, sig, section_ref, sig_ref, sem):
    copies = [
        pltpu.make_async_copy(raw.at[f], section_ref.at[f], sem.at[f]) for f in range(5)
    ] + [pltpu.make_async_copy(sig, sig_ref, sem.at[5])]
    for copy in copies:
        copy.start()
    for copy in copies:
        copy.wait()


def on_device(conserved, panel_cells, panel_counts, time_bins, amplitudes):
    f32 = jnp.float32
    vmem = pl.BlockSpec(memory_space=pltpu.VMEM)
    smem = pl.BlockSpec(memory_space=pltpu.SMEM)
    hbm = pl.BlockSpec(memory_space=pl.ANY)
    dma = pltpu.SemaphoreType.DMA

    def in_hbm(value):
        return pltpu.with_memory_space_constraint(value, pltpu.HBM)

    def in_vmem(value):
        return pltpu.with_memory_space_constraint(value, pltpu.VMEM)

    section, signal = pl.pallas_call(
        step_kernel,
        out_shape=(
            pltpu.VMEM(conserved.shape, f32),
            pltpu.VMEM((2, 64), f32),
        ),
        in_specs=[smem] + [hbm] * 5,
        out_specs=(hbm, vmem),
        scratch_shapes=[
            pltpu.VMEM((5, 8, 64, 128), f32),
            pltpu.VMEM((1, 512), jnp.int32),
            pltpu.VMEM((5, 8, 64, 128), f32),
            pltpu.VMEM((64, 512), jnp.int32),
            pltpu.VMEM((64, 512), f32),
            pltpu.VMEM((8, 1024), f32),
            pltpu.VMEM((12, 5, 64, 128), f32),
            pltpu.VMEM((2, 5, 40, 128), f32),
            pltpu.VMEM((5, 8, 80, 128), f32),
            pltpu.VMEM((512, 128), f32),
            pltpu.VMEM((2, 5, 2, 8, 128), f32),
            pltpu.VMEM((2, 5, 2, 8, 128), f32),
            pltpu.VMEM((6, 5, 8, 128), f32),
            pltpu.VMEM((5, 4, 8, 128), f32),
            pltpu.VMEM((16, 24, 128), f32),
            pltpu.VMEM((16, 24, 128), f32),
            pltpu.VMEM((16, 16, 128), f32),
            pltpu.VMEM((16, 16, 128), f32),
            pltpu.VMEM((16, 32, 128), f32),
            pltpu.VMEM((15, 32, 128), f32),
            pltpu.VMEM((32, 1, 128), f32),
            pltpu.VMEM((31, 1, 128), f32),
            pltpu.VMEM((128, 1024), jnp.bfloat16),
            pltpu.VMEM((128, 1024), jnp.bfloat16),
            dma((4,)),
            dma((8,)),
            dma((8,)),
            dma((8,)),
            dma((4,)),
            dma((4,)),
        ],
        compiler_params=pltpu.CompilerParams(
            collective_id=0, has_side_effects=True, vmem_limit_bytes=24 << 20
        ),
        name="step",
    )(
        panel_counts,
        in_hbm(panel_cells.reshape(1, panel_cells.shape[0])),
        in_hbm(conserved),
        in_hbm(time_bins.T),
        in_hbm(amplitudes.T),
        in_hbm(jnp.asarray(filter_rows())),
    )
    section, signal = pl.pallas_call(
        leave_kernel,
        out_shape=(
            jax.ShapeDtypeStruct(conserved.shape, f32),
            jax.ShapeDtypeStruct((2, 64), f32),
        ),
        in_specs=[hbm, hbm],
        out_specs=(hbm, hbm),
        scratch_shapes=[dma((6,))],
        compiler_params=pltpu.CompilerParams(vmem_limit_bytes=8 << 20),
        name="leave",
    )(in_vmem(section), in_vmem(signal))
    return (section, signal.T)


def solution(mesh):
    placed = (
        P(None, "ax", "az", None),
        P(("ax", "az")),
        P(("ax", "az")),
        P(("ax", "az"), None),
        P(("ax", "az"), None),
    )
    return jax.shard_map(
        on_device,
        mesh=mesh,
        in_specs=placed,
        out_specs=(P(None, "ax", "az", None), P(None, ("ax", "az"))),
        check_vma=False,
    )
```

```python
import math

import jax
import jax.numpy as jnp
import numpy as np
from jax import lax
from jax.experimental import pallas as pl
from jax.experimental.pallas import tpu as pltpu
from jax.sharding import PartitionSpec as P

AZIMUTH = 1024
CYCLES = 8
OBSERVERS = 64
BINS = 1024
MESH = pl.DeviceIdType.MESH

gas_factor = 0.4
time_step = 0.02
ref_pressure = 0.95


def filter_rows():
    n = AZIMUTH
    modes = np.arange(n // 2 + 1, dtype=np.float64)
    lag = np.arange(n)
    factor = np.where((modes == 0) | (modes == n // 2), 1.0, 2.0) / n
    table = np.cos((modes[:, None] * lag[None, :]) % n * (2.0 * np.pi / n))
    rows = np.zeros((CYCLES, 8, n), np.float32)
    for j in range(CYCLES):
        weight = np.exp(-((modes / (4.0 * (j + 1))) ** 8)) * factor
        h = weight @ table
        for r in range(8):
            rows[j, r] = np.roll(h, r)
    return rows


def pieces_of(value, count):
    out = []
    for _ in range(count - 1):
        part = value.astype(jnp.bfloat16)
        out.append(part)
        value = value - part.astype(jnp.float32)
    out.append(value.astype(jnp.bfloat16))
    return out


def dot_t(a, b):
    return lax.dot_general(a, b, (((1,), (1,)), ((), ())), preferred_element_type=jnp.float32)


def axis_ring(n, me, r):
    return lax.rem(me + r, n)


def step_kernel(
    count,
    cells_hbm,
    q_hbm,
    bins_hbm,
    amp_hbm,
    h_hbm,
    out_ref,
    sig_ref,
    raw,
    cells_ref,
    q,
    bins,
    amp,
    h,
    axial,
    relay,
    swirl,
    excess,
    edge_out,
    edge_in,
    inner,
    turned,
    lines_out,
    lines_in,
    smooth_out,
    smooth_in,
    sums,
    sums_in,
    core_in,
    rows,
    rows_in,
    g_hi,
    g_lo,
    load_sem,
    plane_sem,
    near_send,
    near_recv,
    bulk_send,
    bulk_recv,
):
    n_ax, n_az = 32, 16
    ax, az = lax.axis_index("ax"), lax.axis_index("az")

    def remote(source, target, send, recv, ax_to, az_to):
        return pltpu.make_async_remote_copy(
            src_ref=source,
            dst_ref=target,
            send_sem=send,
            recv_sem=recv,
            device_id=(ax_to, az_to),
            device_id_type=MESH,
        )

    loads = [
        pltpu.make_async_copy(cells_hbm, cells_ref, load_sem.at[0]),
        pltpu.make_async_copy(bins_hbm, bins, load_sem.at[1]),
        pltpu.make_async_copy(amp_hbm, amp, load_sem.at[2]),
        pltpu.make_async_copy(h_hbm.at[lax.rem(az, CYCLES)], h, load_sem.at[3]),
    ]

    def plane_load(p):
        return pltpu.make_async_copy(q_hbm.at[:, p], q.at[:, p], plane_sem.at[p])

    for p in range(8):
        plane_load(p).start()
    for copy in loads:
        copy.start()
    for d in range(n_az):
        lines_in[d, 16:24, :] = jnp.zeros((8, 128), jnp.float32)
    barrier = pltpu.get_barrier_semaphore()
    for k in range(1, n_ax):
        r = n_ax // 2 + (k // 2 if k % 2 == 0 else -(k // 2))
        pl.semaphore_signal(
            barrier, inc=1, device_id=(axis_ring(n_ax, ax, r), az), device_id_type=MESH
        )
    for r in range(1, n_az):
        pl.semaphore_signal(
            barrier, inc=1, device_id=(ax, axis_ring(n_az, az, r)), device_id_type=MESH
        )

    lane = lax.broadcasted_iota(jnp.int32, (1, 128), 1)
    radius = lane.astype(jnp.float32) + 0.5
    over_r = 1.0 / radius
    step = jnp.float32(time_step)
    dtheta = 2.0 * math.pi / AZIMUTH
    near = (8.0 / 12.0) * step * over_r
    far = (1.0 / 12.0) * step * over_r
    plus_1 = jnp.where(lane < 127, -near, 0.0)
    minus_1 = jnp.where(lane > 0, near, 0.0)
    plus_2 = jnp.where(lane < 126, far, 0.0)
    minus_2 = jnp.where(lane > 1, -far, 0.0)
    swirl_gain = (-1.0 / 12.0) * step / (radius * dtheta)
    axial_gain = -time_step / 12.0


    def local(p, carry):
        plane_load(p).wait()
        for at in range(0, 64, 16):
            part = pl.ds(at, 16)
            q0, q1, q2, q3, q4 = [q[f, p, part, :] for f in range(5)]
            over = 1.0 / q0
            u, v, w = q1 * over, q2 * over, q3 * over
            pressure = gas_factor * (q4 - 0.5 * (q1 * u + q2 * v + q3 * w))
            excess[pl.ds(pl.multiple_of(p * 64 + at, 16), 16), :] = pressure - ref_pressure
            total = q4 + pressure
            for f, value in enumerate((q1, q1 * u + pressure, q2 * u, q3 * u, total * u)):
                axial[p + 2, f, part, :] = value
            into = pl.ds(at + 8, 16)
            q3w = q3 * w
            for f, value in enumerate((q3, q1 * w, q2 * w, q3w + pressure, total * w)):
                swirl[f, p, into, :] = value
            q3v = q3 * v
            force = step * over_r
            old = (q0, q1, q2 + force * (pressure + q3w), q3 - force * q3v, q4)
            for f, value in enumerate((q2, q1 * v, q2 * v + pressure, q3v, total * v)):
                value = value * radius
                raw[f, p, part, :] = (
                    old[f]
                    + plus_1 * pltpu.roll(value, 127, 1)
                    + minus_1 * pltpu.roll(value, 1, 1)
                    + plus_2 * pltpu.roll(value, 126, 1)
                    + minus_2 * pltpu.roll(value, 2, 1)
                )
        return carry

    lax.fori_loop(0, 8, local, 0)

    for f in range(5):
        for r in range(2):
            edge_out[0, f, r] = swirl[f, :, 8 + r, :]
            edge_out[1, f, r] = swirl[f, :, 70 + r, :]

    def turn_axial(f, carry):
        for a in range(4):
            tile = jnp.concatenate([axial[2 * a + 2, f], axial[2 * a + 3, f]], axis=0)
            inner[a + 1, f] = tile.T[:8]
        return carry

    lax.fori_loop(0, 5, turn_axial, 0)


    @pl.when(ax == 0)
    def _():
        inner[0] = jnp.zeros_like(inner[0])
        axial[0:2] = jnp.zeros((2, 5, 64, 128), jnp.float32)

    @pl.when(ax == n_ax - 1)
    def _():
        inner[5] = jnp.zeros_like(inner[5])
        axial[10:12] = jnp.zeros((2, 5, 64, 128), jnp.float32)

    slots = cells_ref.shape[1]
    loads[0].wait()
    parts = jnp.concatenate(pieces_of(excess[...].T, 3), axis=0)
    cells = cells_ref[...]
    row_hot = lax.broadcasted_iota(jnp.int32, (512, slots), 0) == (cells >> 7)
    row_hot = jnp.where(row_hot, 1.0, 0.0).astype(jnp.bfloat16)
    picked = jnp.dot(parts, row_hot, preferred_element_type=jnp.float32)
    picked = picked[:128] + picked[128:256] + picked[256:]
    lane_hot = lax.broadcasted_iota(jnp.int32, (128, slots), 0) == (cells & 127)
    sampled = jnp.sum(jnp.where(lane_hot, picked, 0.0), axis=0, keepdims=True)
    live = lax.broadcasted_iota(jnp.int32, (1, slots), 1) < count[0]
    sampled = jnp.where(live, sampled, 0.0)
    sixteen = lax.broadcasted_iota(jnp.int32, (16, slots), 0)
    ladder = [(sixteen + 16 * k).astype(jnp.float32).astype(jnp.bfloat16) for k in range(4)]
    one, none = jnp.bfloat16(1.0), jnp.bfloat16(0.0)

    def spread(value, k):
        return jnp.broadcast_to(value[k : k + 1], (16, slots)).astype(jnp.bfloat16)

    loads[1].wait()
    loads[2].wait()

    def group(i, carry):
        ready = []
        for top in range(2):
            at = pl.ds(pl.multiple_of(top * 32 + i * 8, 8), 8)
            b = bins[at, :]
            contrib = sampled * amp[at, :]
            main = contrib.astype(jnp.bfloat16).astype(jnp.float32)
            owner = (((b >> 2) & 7) | ((b & 2) << 2)).astype(jnp.float32)
            rest = (((b & 1) << 5) | (b >> 5)).astype(jnp.float32)
            ready.append((main, contrib - main, owner, rest))
        for k in range(8):
            halves = []
            for main, left_over, owner, rest in ready:
                hit = spread(owner, k) == ladder[0]
                left = jnp.concatenate(
                    [jnp.where(hit, spread(part, k), none) for part in (main, left_over)], axis=0
                )
                place = spread(rest, k)
                right = jnp.concatenate(
                    [jnp.where(place == rung, one, none) for rung in ladder], axis=0
                )
                both = dot_t(left, right)
                halves.append(both[:16] + both[16:])
            sums[:, pl.ds(i * 8 + k, 1), :] = jnp.concatenate(halves, axis=1).reshape(16, 1, 128)
        return carry

    lax.fori_loop(0, 4, group, 0)

    pl.semaphore_wait(barrier, n_ax - 1 + n_az - 1)
    below, above = axis_ring(n_ax, ax, n_ax - 1), axis_ring(n_ax, ax, 1)
    left_az, right_az = axis_ring(n_az, az, n_az - 1), axis_ring(n_az, az, 1)
    edge_low = remote(
        edge_out.at[0], edge_in.at[1], near_send.at[0], near_recv.at[0], ax, left_az
    )
    edge_high = remote(
        edge_out.at[1], edge_in.at[0], near_send.at[1], near_recv.at[1], ax, right_az
    )
    inner_down = remote(inner.at[1], inner.at[5], near_send.at[2], near_recv.at[2], below, az)
    inner_up = remote(inner.at[4], inner.at[0], near_send.at[3], near_recv.at[3], above, az)
    halo_down = remote(
        axial.at[pl.ds(2, 2)],
        axial.at[pl.ds(10, 2)],
        near_send.at[4],
        near_recv.at[4],
        below,
        az,
    )
    halo_up = remote(
        axial.at[pl.ds(8, 2)],
        axial.at[pl.ds(0, 2)],
        near_send.at[5],
        near_recv.at[5],
        above,
        az,
    )
    @pl.when(ax > 0)
    def _():
        inner_down.start()

    @pl.when(ax < n_ax - 1)
    def _():
        inner_up.start()

    edge_low.start()
    edge_high.start()

    @pl.when(jnp.logical_and(ax > 0, ax != n_ax // 2))
    def _():
        halo_down.start()

    @pl.when(jnp.logical_and(ax < n_ax - 1, ax != n_ax // 2 - 1))
    def _():
        halo_up.start()

    core, chip = lax.rem(az, 2), az // 2
    mine, others = pl.ds(core * 8, 8), pl.ds((1 - core) * 8, 8)
    to_core = remote(
        sums.at[others], core_in, near_send.at[8], near_recv.at[8], ax, az + 1 - 2 * core
    )
    to_core.start()

    loads[3].wait()
    first = h[...]
    for k in range(0, 128, 16):
        g = jnp.concatenate(
            [first if k == 0 else pltpu.roll(first, k, 1), pltpu.roll(first, k + 8, 1)], axis=0
        )
        g_hi[k : k + 16], g_lo[k : k + 16] = pieces_of(g, 2)

    for d in range(n_az):
        lines_out[d, 16:24, :] = jnp.zeros((8, 128), jnp.float32)

    def turn_lines(f, carry):
        for a in range(4):
            tile = jnp.concatenate([raw[f, 2 * a], raw[f, 2 * a + 1]], axis=0)
            turned[f, a] = tile.T[:8]
            tile = jnp.concatenate([swirl[f, 2 * a, 8:72, :], swirl[f, 2 * a + 1, 8:72, :]], axis=0)
            lines_out[
                pl.ds((a // 2) * 8, 8), pl.ds(10 + f * 2 + a % 2, 1), :
            ] = tile.T[:8].reshape(8, 1, 128)
        return carry

    lax.fori_loop(0, 5, turn_lines, 0)
    to_core.wait_recv()
    sums[mine] = sums[mine] + core_in[...]
    for r in range(1, 8):
        other = axis_ring(8, chip, r)
        remote(
            sums.at[core * 8 + other],
            sums_in.at[r - 1],
            bulk_send.at[0],
            bulk_recv.at[0],
            ax,
            other * 2 + core,
        ).start()
    all_sums = remote(
        sums.at[pl.ds(0, 7)], sums_in, bulk_send.at[0], bulk_recv.at[0], ax, right_az
    )

    @pl.when(ax < n_ax - 1)
    def _():
        inner_down.wait_recv()

    @pl.when(ax > 0)
    def _():
        inner_up.wait_recv()

    upper = lane >= 64
    for f in range(5):
        for a in range(4):
            before, now, after = inner[a, f], inner[a + 1, f], inner[a + 2, f]
            next_1 = pltpu.roll(jnp.where(upper, now, after), 64, 1)
            last_1 = pltpu.roll(jnp.where(upper, before, now), 64, 1)
            line = turned[f, a] + axial_gain * (8.0 * (next_1 - last_1) - (after - before))
            at = (a // 2) * 8
            row = f * 2 + a % 2
            lines_out[at : at + 8, row : row + 1, :] = line.reshape(8, 1, 128)
    filled = pl.ds(0, 20)
    for r in range(1, n_az):
        peer = axis_ring(n_az, az, r)
        remote(
            lines_out.at[peer, filled], lines_in.at[az, filled], bulk_send.at[1], bulk_recv.at[1], ax, peer
        ).start()
    most = pl.ds(0, 15)
    all_lines = remote(
        lines_out.at[most, filled], lines_in.at[most, filled], bulk_send.at[1], bulk_recv.at[1], ax, right_az
    )

    lines_in[az] = lines_out[az]
    middle = n_ax // 2
    pair_up, land_up = pl.ds(8, 2), pl.ds(0, 2)
    routes = []
    for by, start, size, place, slot in (
        (n_ax - 1, 8, 24, 0, 6),
        (n_ax - 1, 32, 16, 24, 7),
        (middle + 1, 48, 8, 0, 6),
        (n_ax - 2, 56, 8, 0, 6),
    ):
        share = pl.ds(start, size)
        stop = relay.at[:, :, pl.ds(place, size), :]
        leg = remote(
            axial.at[pair_up, :, share, :], stop, near_send.at[5], near_recv.at[slot], by, az
        )
        forward = remote(
            stop, axial.at[land_up, :, share, :], near_send.at[slot], near_recv.at[5], middle, az
        )
        routes.append((middle - 1, by, leg, forward))
    share = pl.ds(0, 8)
    up_direct = remote(
        axial.at[pair_up, :, share, :],
        axial.at[land_up, :, share, :],
        near_send.at[5],
        near_recv.at[5],
        middle,
        az,
    )
    for begins, _, leg, _ in routes:

        @pl.when(ax == begins)
        def _():
            leg.start()

    edge_low.wait_recv()
    edge_high.wait_recv()
    for f in range(5):
        for r in range(2):
            swirl[f, :, 6 + r, :] = edge_in[0, f, r]
            swirl[f, :, 72 + r, :] = edge_in[1, f, r]

    def around(p, carry):
        for f in range(5):
            raw[f, p] = raw[f, p] + swirl_gain * (
                8.0 * (swirl[f, p, 9:73, :] - swirl[f, p, 7:71, :])
                - (swirl[f, p, 10:74, :] - swirl[f, p, 6:70, :])
            )
        return carry

    lax.fori_loop(0, 8, around, 0)

    all_sums.wait_recv()
    total = sums[core * 8 + chip]
    for r in range(1, 8):
        total = total + sums_in[r - 1]
    flipped = total.T
    rows[...] = jnp.concatenate(
        [flipped[(top * 2 + e) * 32 : (top * 2 + e) * 32 + 32] for e in range(2) for top in range(2)],
        axis=1,
    ).reshape(n_ax, 1, 128)
    for r in range(1, n_ax):
        peer = axis_ring(n_ax, ax, r)
        remote(rows.at[peer], rows_in.at[r - 1], bulk_send.at[2], bulk_recv.at[2], peer, az).start()
    all_rows = remote(
        rows.at[pl.ds(0, 31)], rows_in, bulk_send.at[2], bulk_recv.at[2], above, az
    )

    @pl.when(ax == middle - 1)
    def _():
        up_direct.start()

    @pl.when(ax == middle)
    def _():
        halo_down.start()

    def relay_on(some):
        for _, by, leg, forward in some:

            @pl.when(ax == by)
            def _():
                leg.wait_recv()
                forward.start()

    relay_on(routes[:1])
    all_lines.wait_recv()
    relay_on(routes[1:2])

    low, high = [], []
    for s in range(0, n_az, 2):
        one, two = lines_in[s], lines_in[s + 1]
        low.append(jnp.where(upper, pltpu.roll(two, 64, 1), one))
        high.append(jnp.where(upper, two, pltpu.roll(one, 64, 1)))
    cycle = lax.rem(az, CYCLES).astype(jnp.float32) + 0.5
    gain = jnp.full((1, 128), -time_step / 12.0 / dtheta, jnp.float32) / cycle
    gain = gain[:, :1]

    def completed(both):
        swirls = both[8:24]
        change = 8.0 * (
            pltpu.roll(swirls, AZIMUTH - 1, 1) - pltpu.roll(swirls, 1, 1)
        ) - (pltpu.roll(swirls, AZIMUTH - 2, 1) - pltpu.roll(swirls, 2, 1))
        return both[:16] + gain * pltpu.roll(change, 14, 0)

    x = jnp.concatenate(
        [completed(jnp.concatenate(low, axis=1)), completed(jnp.concatenate(high, axis=1))], axis=0
    )

    def turns(part):
        return jnp.concatenate(
            [
                part
                if a == 0
                else jnp.concatenate([part[:, 128 * a :], part[:, : 128 * a]], axis=1)
                for a in range(8)
            ],
            axis=0,
        )

    x_hi, x_lo = [turns(part) for part in pieces_of(x, 2)]
    k_hi, k_lo = g_hi[...], g_lo[...]
    y = dot_t(x_hi, k_hi) + (dot_t(x_lo, k_hi) + dot_t(x_hi, k_lo))
    for a in range(8):
        one, two = y[32 * a : 32 * a + 16], y[32 * a + 16 : 32 * a + 32]
        smooth_out[2 * a] = jnp.where(upper, pltpu.roll(two, 64, 1), one)
        smooth_out[2 * a + 1] = jnp.where(upper, two, pltpu.roll(one, 64, 1))
    used = pl.ds(0, 10)
    for r in range(1, n_az):
        peer = axis_ring(n_az, az, r)
        remote(
            smooth_out.at[peer, used], smooth_in.at[az, used], bulk_send.at[3], bulk_recv.at[3], ax, peer
        ).start()
    all_smooth = remote(
        smooth_out.at[most, used], smooth_in.at[most, used], bulk_send.at[3], bulk_recv.at[3], ax, right_az
    )
    smooth_in[az] = smooth_out[az]
    relay_on(routes[2:])
    @pl.when(ax < n_ax - 1)
    def _():
        halo_down.wait_recv()

    @pl.when(ax > 0)
    def _():
        halo_up.wait_recv()

    def along(p, carry):
        for f in range(5):
            raw[f, p] = raw[f, p] + axial_gain * (
                8.0 * (axial[p + 3, f] - axial[p + 1, f]) - (axial[p + 4, f] - axial[p, f])
            )
        return carry

    lax.fori_loop(0, 8, along, 0)

    all_smooth.wait_recv()
    cycles = lane < 8

    def turn_back(f, carry):
        for a in range(4):
            line = smooth_in[
                pl.ds((a // 2) * 8, 8), pl.ds(f * 2 + a % 2, 1), :
            ].reshape(8, 128)
            tile = jnp.concatenate([line, jnp.zeros((120, 128), jnp.float32)], axis=0).T
            for b in range(2):
                raw[f, 2 * a + b] = jnp.where(
                    cycles, tile[64 * b : 64 * b + 64], raw[f, 2 * a + b]
                )
        return carry

    lax.fori_loop(0, 5, turn_back, 0)
    section_copy = pltpu.make_async_copy(raw, out_ref, load_sem.at[0])
    section_copy.start()
    all_rows.wait_recv()
    total = rows[ax]
    for r in range(1, n_ax):
        total = total + rows_in[r - 1]
    sig_ref[...] = jnp.concatenate([total[:, :64], total[:, 64:]], axis=0)

    section_copy.wait()
    for copy in (edge_low, edge_high, to_core, all_sums, all_lines, all_rows, all_smooth):
        copy.wait_send()

    @pl.when(ax > 0)
    def _():
        inner_down.wait_send()
        halo_down.wait_send()

    @pl.when(ax < n_ax - 1)
    def _():
        inner_up.wait_send()
        halo_up.wait_send()

    for _, by, _, forward in routes:

        @pl.when(ax == by)
        def _():
            forward.wait_send()


def leave_kernel(raw, sig, section_ref, sig_ref, sem):
    copies = [
        pltpu.make_async_copy(raw.at[f], section_ref.at[f], sem.at[f]) for f in range(5)
    ] + [pltpu.make_async_copy(sig, sig_ref, sem.at[5])]
    for copy in copies:
        copy.start()
    for copy in copies:
        copy.wait()


def on_device(conserved, panel_cells, panel_counts, time_bins, amplitudes):
    f32 = jnp.float32
    vmem = pl.BlockSpec(memory_space=pltpu.VMEM)
    smem = pl.BlockSpec(memory_space=pltpu.SMEM)
    hbm = pl.BlockSpec(memory_space=pl.ANY)
    dma = pltpu.SemaphoreType.DMA

    def in_hbm(value):
        return pltpu.with_memory_space_constraint(value, pltpu.HBM)

    def in_vmem(value):
        return pltpu.with_memory_space_constraint(value, pltpu.VMEM)

    section, signal = pl.pallas_call(
        step_kernel,
        out_shape=(
            pltpu.VMEM(conserved.shape, f32),
            pltpu.VMEM((2, 64), f32),
        ),
        in_specs=[smem] + [hbm] * 5,
        out_specs=(hbm, vmem),
        scratch_shapes=[
            pltpu.VMEM((5, 8, 64, 128), f32),
            pltpu.VMEM((1, 512), jnp.int32),
            pltpu.VMEM((5, 8, 64, 128), f32),
            pltpu.VMEM((64, 512), jnp.int32),
            pltpu.VMEM((64, 512), f32),
            pltpu.VMEM((8, 1024), f32),
            pltpu.VMEM((12, 5, 64, 128), f32),
            pltpu.VMEM((2, 5, 40, 128), f32),
            pltpu.VMEM((5, 8, 80, 128), f32),
            pltpu.VMEM((512, 128), f32),
            pltpu.VMEM((2, 5, 2, 8, 128), f32),
            pltpu.VMEM((2, 5, 2, 8, 128), f32),
            pltpu.VMEM((6, 5, 8, 128), f32),
            pltpu.VMEM((5, 4, 8, 128), f32),
            pltpu.VMEM((16, 24, 128), f32),
            pltpu.VMEM((16, 24, 128), f32),
            pltpu.VMEM((16, 16, 128), f32),
            pltpu.VMEM((16, 16, 128), f32),
            pltpu.VMEM((16, 32, 128), f32),
            pltpu.VMEM((7, 32, 128), f32),
            pltpu.VMEM((8, 32, 128), f32),
            pltpu.VMEM((32, 1, 128), f32),
            pltpu.VMEM((31, 1, 128), f32),
            pltpu.VMEM((128, 1024), jnp.bfloat16),
            pltpu.VMEM((128, 1024), jnp.bfloat16),
            dma((4,)),
            dma((8,)),
            dma((9,)),
            dma((9,)),
            dma((4,)),
            dma((4,)),
        ],
        compiler_params=pltpu.CompilerParams(
            collective_id=0, has_side_effects=True, vmem_limit_bytes=24 << 20
        ),
        name="step",
    )(
        panel_counts,
        in_hbm(panel_cells.reshape(1, panel_cells.shape[0])),
        in_hbm(conserved),
        in_hbm(time_bins.T),
        in_hbm(amplitudes.T),
        in_hbm(jnp.asarray(filter_rows())),
    )
    section, signal = pl.pallas_call(
        leave_kernel,
        out_shape=(
            jax.ShapeDtypeStruct(conserved.shape, f32),
            jax.ShapeDtypeStruct((2, 64), f32),
        ),
        in_specs=[hbm, hbm],
        out_specs=(hbm, hbm),
        scratch_shapes=[dma((6,))],
        compiler_params=pltpu.CompilerParams(vmem_limit_bytes=8 << 20),
        name="leave",
    )(in_vmem(section), in_vmem(signal))
    return (section, signal.T)


def solution(mesh):
    placed = (
        P(None, "ax", "az", None),
        P(("ax", "az")),
        P(("ax", "az")),
        P(("ax", "az"), None),
        P(("ax", "az"), None),
    )
    return jax.shard_map(
        on_device,
        mesh=mesh,
        in_specs=placed,
        out_specs=(P(None, "ax", "az", None), P(None, ("ax", "az"))),
        check_vma=False,
    )
```

```python
import math

import jax
import jax.numpy as jnp
import numpy as np
from jax import lax
from jax.experimental import pallas as pl
from jax.experimental.pallas import tpu as pltpu
from jax.sharding import PartitionSpec as P

AZIMUTH = 1024
CYCLES = 8
OBSERVERS = 64
BINS = 1024
MESH = pl.DeviceIdType.MESH

gas_factor = 0.4
time_step = 0.02
ref_pressure = 0.95


def filter_rows():
    n = AZIMUTH
    modes = np.arange(n // 2 + 1, dtype=np.float64)
    lag = np.arange(n)
    factor = np.where((modes == 0) | (modes == n // 2), 1.0, 2.0) / n
    table = np.cos((modes[:, None] * lag[None, :]) % n * (2.0 * np.pi / n))
    rows = np.zeros((CYCLES, 8, n), np.float32)
    for j in range(CYCLES):
        weight = np.exp(-((modes / (4.0 * (j + 1))) ** 8)) * factor
        h = weight @ table
        for r in range(8):
            rows[j, r] = np.roll(h, r)
    return rows


def pieces_of(value, count):
    out = []
    for _ in range(count - 1):
        part = value.astype(jnp.bfloat16)
        out.append(part)
        value = value - part.astype(jnp.float32)
    out.append(value.astype(jnp.bfloat16))
    return out


def dot_t(a, b):
    return lax.dot_general(a, b, (((1,), (1,)), ((), ())), preferred_element_type=jnp.float32)


def axis_ring(n, me, r):
    return lax.rem(me + r, n)


def step_kernel(
    count,
    cells_hbm,
    q_hbm,
    bins_hbm,
    amp_hbm,
    h_hbm,
    out_ref,
    sig_ref,
    raw,
    cells_ref,
    q,
    bins,
    amp,
    h,
    axial,
    relay,
    swirl,
    excess,
    edge_out,
    edge_in,
    inner,
    turned,
    lines_out,
    lines_in,
    smooth_out,
    smooth_in,
    sums,
    sums_in,
    core_in,
    rows,
    rows_in,
    g_hi,
    g_lo,
    load_sem,
    plane_sem,
    near_send,
    near_recv,
    bulk_send,
    bulk_recv,
):
    n_ax, n_az = 32, 16
    ax, az = lax.axis_index("ax"), lax.axis_index("az")

    def remote(source, target, send, recv, ax_to, az_to):
        return pltpu.make_async_remote_copy(
            src_ref=source,
            dst_ref=target,
            send_sem=send,
            recv_sem=recv,
            device_id=(ax_to, az_to),
            device_id_type=MESH,
        )

    loads = [
        pltpu.make_async_copy(cells_hbm, cells_ref, load_sem.at[0]),
        pltpu.make_async_copy(bins_hbm, bins, load_sem.at[1]),
        pltpu.make_async_copy(amp_hbm, amp, load_sem.at[2]),
        pltpu.make_async_copy(h_hbm.at[lax.rem(az, CYCLES)], h, load_sem.at[3]),
    ]

    def plane_load(p):
        return pltpu.make_async_copy(q_hbm.at[:, p], q.at[:, p], plane_sem.at[p])

    for p in range(8):
        plane_load(p).start()
    for copy in loads:
        copy.start()
    for d in range(n_az):
        lines_in[d, 16:24, :] = jnp.zeros((8, 128), jnp.float32)
    barrier = pltpu.get_barrier_semaphore()
    for k in range(1, n_ax):
        r = n_ax // 2 + (k // 2 if k % 2 == 0 else -(k // 2))
        pl.semaphore_signal(
            barrier, inc=1, device_id=(axis_ring(n_ax, ax, r), az), device_id_type=MESH
        )
    for r in range(1, n_az):
        pl.semaphore_signal(
            barrier, inc=1, device_id=(ax, axis_ring(n_az, az, r)), device_id_type=MESH
        )

    lane = lax.broadcasted_iota(jnp.int32, (1, 128), 1)
    radius = lane.astype(jnp.float32) + 0.5
    over_r = 1.0 / radius
    step = jnp.float32(time_step)
    dtheta = 2.0 * math.pi / AZIMUTH
    near = (8.0 / 12.0) * step * over_r
    far = (1.0 / 12.0) * step * over_r
    plus_1 = jnp.where(lane < 127, -near, 0.0)
    minus_1 = jnp.where(lane > 0, near, 0.0)
    plus_2 = jnp.where(lane < 126, far, 0.0)
    minus_2 = jnp.where(lane > 1, -far, 0.0)
    swirl_gain = (-1.0 / 12.0) * step / (radius * dtheta)
    axial_gain = -time_step / 12.0


    def local(p, carry):
        plane_load(p).wait()
        for at in range(0, 64, 16):
            part = pl.ds(at, 16)
            q0, q1, q2, q3, q4 = [q[f, p, part, :] for f in range(5)]
            over = 1.0 / q0
            u, v, w = q1 * over, q2 * over, q3 * over
            pressure = gas_factor * (q4 - 0.5 * (q1 * u + q2 * v + q3 * w))
            excess[pl.ds(pl.multiple_of(p * 64 + at, 16), 16), :] = pressure - ref_pressure
            total = q4 + pressure
            for f, value in enumerate((q1, q1 * u + pressure, q2 * u, q3 * u, total * u)):
                axial[p + 2, f, part, :] = value
            into = pl.ds(at + 8, 16)
            q3w = q3 * w
            for f, value in enumerate((q3, q1 * w, q2 * w, q3w + pressure, total * w)):
                swirl[f, p, into, :] = value
            q3v = q3 * v
            force = step * over_r
            old = (q0, q1, q2 + force * (pressure + q3w), q3 - force * q3v, q4)
            for f, value in enumerate((q2, q1 * v, q2 * v + pressure, q3v, total * v)):
                value = value * radius
                raw[f, p, part, :] = (
                    old[f]
                    + plus_1 * pltpu.roll(value, 127, 1)
                    + minus_1 * pltpu.roll(value, 1, 1)
                    + plus_2 * pltpu.roll(value, 126, 1)
                    + minus_2 * pltpu.roll(value, 2, 1)
                )
        return carry

    lax.fori_loop(0, 8, local, 0)

    for f in range(5):
        for r in range(2):
            edge_out[0, f, r] = swirl[f, :, 8 + r, :]
            edge_out[1, f, r] = swirl[f, :, 70 + r, :]

    def turn_axial(f, carry):
        for a in range(4):
            tile = jnp.concatenate([axial[2 * a + 2, f], axial[2 * a + 3, f]], axis=0)
            inner[a + 1, f] = tile.T[:8]
        return carry

    lax.fori_loop(0, 5, turn_axial, 0)


    @pl.when(ax == 0)
    def _():
        inner[0] = jnp.zeros_like(inner[0])
        axial[0:2] = jnp.zeros((2, 5, 64, 128), jnp.float32)

    @pl.when(ax == n_ax - 1)
    def _():
        inner[5] = jnp.zeros_like(inner[5])
        axial[10:12] = jnp.zeros((2, 5, 64, 128), jnp.float32)

    slots = cells_ref.shape[1]
    loads[0].wait()
    parts = jnp.concatenate(pieces_of(excess[...].T, 3), axis=0)
    cells = cells_ref[...]
    row_hot = lax.broadcasted_iota(jnp.int32, (512, slots), 0) == (cells >> 7)
    row_hot = jnp.where(row_hot, 1.0, 0.0).astype(jnp.bfloat16)
    picked = jnp.dot(parts, row_hot, preferred_element_type=jnp.float32)
    picked = picked[:128] + picked[128:256] + picked[256:]
    lane_hot = lax.broadcasted_iota(jnp.int32, (128, slots), 0) == (cells & 127)
    sampled = jnp.sum(jnp.where(lane_hot, picked, 0.0), axis=0, keepdims=True)
    live = lax.broadcasted_iota(jnp.int32, (1, slots), 1) < count[0]
    sampled = jnp.where(live, sampled, 0.0)
    sixteen = lax.broadcasted_iota(jnp.int32, (16, slots), 0)
    ladder = [(sixteen + 16 * k).astype(jnp.float32).astype(jnp.bfloat16) for k in range(4)]
    one, none = jnp.bfloat16(1.0), jnp.bfloat16(0.0)

    def spread(value, k):
        return jnp.broadcast_to(value[k : k + 1], (16, slots)).astype(jnp.bfloat16)

    loads[1].wait()
    loads[2].wait()

    def group(i, carry):
        ready = []
        for top in range(2):
            at = pl.ds(pl.multiple_of(top * 32 + i * 8, 8), 8)
            b = bins[at, :]
            contrib = sampled * amp[at, :]
            main = contrib.astype(jnp.bfloat16).astype(jnp.float32)
            owner = (((b >> 2) & 7) | ((b & 2) << 2)).astype(jnp.float32)
            rest = (((b & 1) << 5) | (b >> 5)).astype(jnp.float32)
            ready.append((main, contrib - main, owner, rest))
        for k in range(8):
            halves = []
            for main, left_over, owner, rest in ready:
                hit = spread(owner, k) == ladder[0]
                left = jnp.concatenate(
                    [jnp.where(hit, spread(part, k), none) for part in (main, left_over)], axis=0
                )
                place = spread(rest, k)
                right = jnp.concatenate(
                    [jnp.where(place == rung, one, none) for rung in ladder], axis=0
                )
                both = dot_t(left, right)
                halves.append(both[:16] + both[16:])
            sums[:, pl.ds(i * 8 + k, 1), :] = jnp.concatenate(halves, axis=1).reshape(16, 1, 128)
        return carry

    lax.fori_loop(0, 4, group, 0)

    pl.semaphore_wait(barrier, n_ax - 1 + n_az - 1)
    below, above = axis_ring(n_ax, ax, n_ax - 1), axis_ring(n_ax, ax, 1)
    left_az, right_az = axis_ring(n_az, az, n_az - 1), axis_ring(n_az, az, 1)
    edge_low = remote(
        edge_out.at[0], edge_in.at[1], near_send.at[0], near_recv.at[0], ax, left_az
    )
    edge_high = remote(
        edge_out.at[1], edge_in.at[0], near_send.at[1], near_recv.at[1], ax, right_az
    )
    inner_down = remote(inner.at[1], inner.at[5], near_send.at[2], near_recv.at[2], below, az)
    inner_up = remote(inner.at[4], inner.at[0], near_send.at[3], near_recv.at[3], above, az)
    halo_down = remote(
        axial.at[pl.ds(2, 2)],
        axial.at[pl.ds(10, 2)],
        near_send.at[4],
        near_recv.at[4],
        below,
        az,
    )
    halo_up = remote(
        axial.at[pl.ds(8, 2)],
        axial.at[pl.ds(0, 2)],
        near_send.at[5],
        near_recv.at[5],
        above,
        az,
    )
    @pl.when(ax > 0)
    def _():
        inner_down.start()

    @pl.when(ax < n_ax - 1)
    def _():
        inner_up.start()

    edge_low.start()
    edge_high.start()

    @pl.when(jnp.logical_and(ax > 0, ax != n_ax // 2))
    def _():
        halo_down.start()

    @pl.when(jnp.logical_and(ax < n_ax - 1, ax != n_ax // 2 - 1))
    def _():
        halo_up.start()

    core, chip = lax.rem(az, 2), az // 2
    mine, others = pl.ds(core * 8, 8), pl.ds((1 - core) * 8, 8)
    to_core = remote(
        sums.at[others], core_in, near_send.at[8], near_recv.at[8], ax, az + 1 - 2 * core
    )
    to_core.start()

    loads[3].wait()
    first = h[...]
    for k in range(0, 128, 16):
        g = jnp.concatenate(
            [first if k == 0 else pltpu.roll(first, k, 1), pltpu.roll(first, k + 8, 1)], axis=0
        )
        g_hi[k : k + 16], g_lo[k : k + 16] = pieces_of(g, 2)

    for d in range(n_az):
        lines_out[d, 16:24, :] = jnp.zeros((8, 128), jnp.float32)

    def turn_lines(f, carry):
        for a in range(4):
            tile = jnp.concatenate([raw[f, 2 * a], raw[f, 2 * a + 1]], axis=0)
            turned[f, a] = tile.T[:8]
            tile = jnp.concatenate([swirl[f, 2 * a, 8:72, :], swirl[f, 2 * a + 1, 8:72, :]], axis=0)
            lines_out[
                pl.ds((a // 2) * 8, 8), pl.ds(10 + f * 2 + a % 2, 1), :
            ] = tile.T[:8].reshape(8, 1, 128)
        return carry

    lax.fori_loop(0, 5, turn_lines, 0)
    to_core.wait_recv()
    sums[mine] = sums[mine] + core_in[...]
    for r in range(1, 8):
        other = axis_ring(8, chip, r)
        remote(
            sums.at[core * 8 + other],
            sums_in.at[r - 1],
            bulk_send.at[0],
            bulk_recv.at[0],
            ax,
            other * 2 + core,
        ).start()
    all_sums = remote(
        sums.at[pl.ds(0, 7)], sums_in, bulk_send.at[0], bulk_recv.at[0], ax, right_az
    )

    @pl.when(ax < n_ax - 1)
    def _():
        inner_down.wait_recv()

    @pl.when(ax > 0)
    def _():
        inner_up.wait_recv()

    upper = lane >= 64
    for f in range(5):
        for a in range(4):
            before, now, after = inner[a, f], inner[a + 1, f], inner[a + 2, f]
            next_1 = pltpu.roll(jnp.where(upper, now, after), 64, 1)
            last_1 = pltpu.roll(jnp.where(upper, before, now), 64, 1)
            line = turned[f, a] + axial_gain * (8.0 * (next_1 - last_1) - (after - before))
            at = (a // 2) * 8
            row = f * 2 + a % 2
            lines_out[at : at + 8, row : row + 1, :] = line.reshape(8, 1, 128)
    filled = pl.ds(0, 20)
    for r in range(1, n_az):
        peer = axis_ring(n_az, az, r)
        remote(
            lines_out.at[peer, filled], lines_in.at[az, filled], bulk_send.at[1], bulk_recv.at[1], ax, peer
        ).start()
    most = pl.ds(0, 15)
    all_lines = remote(
        lines_out.at[most, filled], lines_in.at[most, filled], bulk_send.at[1], bulk_recv.at[1], ax, right_az
    )

    lines_in[az] = lines_out[az]
    middle = n_ax // 2
    pair_up, land_up = pl.ds(8, 2), pl.ds(0, 2)
    routes = []
    for by, start, size, place, slot in (
        (n_ax - 1, 16, 24, 0, 6),
        (n_ax - 1, 40, 8, 24, 7),
        (middle + 1, 48, 8, 0, 6),
        (n_ax - 2, 56, 8, 0, 6),
    ):
        share = pl.ds(start, size)
        stop = relay.at[:, :, pl.ds(place, size), :]
        leg = remote(
            axial.at[pair_up, :, share, :], stop, near_send.at[5], near_recv.at[slot], by, az
        )
        forward = remote(
            stop, axial.at[land_up, :, share, :], near_send.at[slot], near_recv.at[5], middle, az
        )
        routes.append((middle - 1, by, leg, forward))
    share = pl.ds(0, 16)
    up_direct = remote(
        axial.at[pair_up, :, share, :],
        axial.at[land_up, :, share, :],
        near_send.at[5],
        near_recv.at[5],
        middle,
        az,
    )
    for begins, _, leg, _ in routes:

        @pl.when(ax == begins)
        def _():
            leg.start()

    edge_low.wait_recv()
    edge_high.wait_recv()
    for f in range(5):
        for r in range(2):
            swirl[f, :, 6 + r, :] = edge_in[0, f, r]
            swirl[f, :, 72 + r, :] = edge_in[1, f, r]

    def around(p, carry):
        for f in range(5):
            raw[f, p] = raw[f, p] + swirl_gain * (
                8.0 * (swirl[f, p, 9:73, :] - swirl[f, p, 7:71, :])
                - (swirl[f, p, 10:74, :] - swirl[f, p, 6:70, :])
            )
        return carry

    lax.fori_loop(0, 8, around, 0)

    all_sums.wait_recv()
    total = sums[core * 8 + chip]
    for r in range(1, 8):
        total = total + sums_in[r - 1]
    flipped = total.T
    rows[...] = jnp.concatenate(
        [flipped[(top * 2 + e) * 32 : (top * 2 + e) * 32 + 32] for e in range(2) for top in range(2)],
        axis=1,
    ).reshape(n_ax, 1, 128)
    for r in range(1, n_ax):
        peer = axis_ring(n_ax, ax, r)
        remote(rows.at[peer], rows_in.at[r - 1], bulk_send.at[2], bulk_recv.at[2], peer, az).start()
    all_rows = remote(
        rows.at[pl.ds(0, 31)], rows_in, bulk_send.at[2], bulk_recv.at[2], above, az
    )

    @pl.when(ax == middle - 1)
    def _():
        up_direct.start()

    @pl.when(ax == middle)
    def _():
        halo_down.start()

    def relay_on(some):
        for _, by, leg, forward in some:

            @pl.when(ax == by)
            def _():
                leg.wait_recv()
                forward.start()

    relay_on(routes[:1])
    all_lines.wait_recv()
    relay_on(routes[1:2])

    low, high = [], []
    for s in range(0, n_az, 2):
        one, two = lines_in[s], lines_in[s + 1]
        low.append(jnp.where(upper, pltpu.roll(two, 64, 1), one))
        high.append(jnp.where(upper, two, pltpu.roll(one, 64, 1)))
    cycle = lax.rem(az, CYCLES).astype(jnp.float32) + 0.5
    gain = jnp.full((1, 128), -time_step / 12.0 / dtheta, jnp.float32) / cycle
    gain = gain[:, :1]

    def completed(both):
        swirls = both[8:24]
        change = 8.0 * (
            pltpu.roll(swirls, AZIMUTH - 1, 1) - pltpu.roll(swirls, 1, 1)
        ) - (pltpu.roll(swirls, AZIMUTH - 2, 1) - pltpu.roll(swirls, 2, 1))
        return both[:16] + gain * pltpu.roll(change, 14, 0)

    x = jnp.concatenate(
        [completed(jnp.concatenate(low, axis=1)), completed(jnp.concatenate(high, axis=1))], axis=0
    )

    def turns(part):
        return jnp.concatenate(
            [
                part
                if a == 0
                else jnp.concatenate([part[:, 128 * a :], part[:, : 128 * a]], axis=1)
                for a in range(8)
            ],
            axis=0,
        )

    x_hi, x_lo = [turns(part) for part in pieces_of(x, 2)]
    k_hi, k_lo = g_hi[...], g_lo[...]
    y = dot_t(x_hi, k_hi) + (dot_t(x_lo, k_hi) + dot_t(x_hi, k_lo))
    for a in range(8):
        one, two = y[32 * a : 32 * a + 16], y[32 * a + 16 : 32 * a + 32]
        smooth_out[2 * a] = jnp.where(upper, pltpu.roll(two, 64, 1), one)
        smooth_out[2 * a + 1] = jnp.where(upper, two, pltpu.roll(one, 64, 1))
    used = pl.ds(0, 10)
    for r in range(1, n_az):
        peer = axis_ring(n_az, az, r)
        remote(
            smooth_out.at[peer, used], smooth_in.at[az, used], bulk_send.at[3], bulk_recv.at[3], ax, peer
        ).start()
    all_smooth = remote(
        smooth_out.at[most, used], smooth_in.at[most, used], bulk_send.at[3], bulk_recv.at[3], ax, right_az
    )
    smooth_in[az] = smooth_out[az]
    relay_on(routes[2:])
    @pl.when(ax < n_ax - 1)
    def _():
        halo_down.wait_recv()

    @pl.when(ax > 0)
    def _():
        halo_up.wait_recv()

    def along(p, carry):
        for f in range(5):
            raw[f, p] = raw[f, p] + axial_gain * (
                8.0 * (axial[p + 3, f] - axial[p + 1, f]) - (axial[p + 4, f] - axial[p, f])
            )
        return carry

    lax.fori_loop(0, 8, along, 0)

    all_smooth.wait_recv()
    cycles = lane < 8

    def turn_back(f, carry):
        for a in range(4):
            line = smooth_in[
                pl.ds((a // 2) * 8, 8), pl.ds(f * 2 + a % 2, 1), :
            ].reshape(8, 128)
            tile = jnp.concatenate([line, jnp.zeros((120, 128), jnp.float32)], axis=0).T
            for b in range(2):
                raw[f, 2 * a + b] = jnp.where(
                    cycles, tile[64 * b : 64 * b + 64], raw[f, 2 * a + b]
                )
        return carry

    lax.fori_loop(0, 5, turn_back, 0)
    section_copy = pltpu.make_async_copy(raw, out_ref, load_sem.at[0])
    section_copy.start()
    all_rows.wait_recv()
    total = rows[ax]
    for r in range(1, n_ax):
        total = total + rows_in[r - 1]
    sig_ref[...] = jnp.concatenate([total[:, :64], total[:, 64:]], axis=0)

    section_copy.wait()
    for copy in (edge_low, edge_high, to_core, all_sums, all_lines, all_rows, all_smooth):
        copy.wait_send()

    @pl.when(ax > 0)
    def _():
        inner_down.wait_send()
        halo_down.wait_send()

    @pl.when(ax < n_ax - 1)
    def _():
        inner_up.wait_send()
        halo_up.wait_send()

    for _, by, _, forward in routes:

        @pl.when(ax == by)
        def _():
            forward.wait_send()


def leave_kernel(raw, sig, section_ref, sig_ref, sem):
    copies = [
        pltpu.make_async_copy(raw.at[f], section_ref.at[f], sem.at[f]) for f in range(5)
    ] + [pltpu.make_async_copy(sig, sig_ref, sem.at[5])]
    for copy in copies:
        copy.start()
    for copy in copies:
        copy.wait()


def on_device(conserved, panel_cells, panel_counts, time_bins, amplitudes):
    f32 = jnp.float32
    vmem = pl.BlockSpec(memory_space=pltpu.VMEM)
    smem = pl.BlockSpec(memory_space=pltpu.SMEM)
    hbm = pl.BlockSpec(memory_space=pl.ANY)
    dma = pltpu.SemaphoreType.DMA

    def in_hbm(value):
        return pltpu.with_memory_space_constraint(value, pltpu.HBM)

    def in_vmem(value):
        return pltpu.with_memory_space_constraint(value, pltpu.VMEM)

    section, signal = pl.pallas_call(
        step_kernel,
        out_shape=(
            pltpu.VMEM(conserved.shape, f32),
            pltpu.VMEM((2, 64), f32),
        ),
        in_specs=[smem] + [hbm] * 5,
        out_specs=(hbm, vmem),
        scratch_shapes=[
            pltpu.VMEM((5, 8, 64, 128), f32),
            pltpu.VMEM((1, 512), jnp.int32),
            pltpu.VMEM((5, 8, 64, 128), f32),
            pltpu.VMEM((64, 512), jnp.int32),
            pltpu.VMEM((64, 512), f32),
            pltpu.VMEM((8, 1024), f32),
            pltpu.VMEM((12, 5, 64, 128), f32),
            pltpu.VMEM((2, 5, 32, 128), f32),
            pltpu.VMEM((5, 8, 80, 128), f32),
            pltpu.VMEM((512, 128), f32),
            pltpu.VMEM((2, 5, 2, 8, 128), f32),
            pltpu.VMEM((2, 5, 2, 8, 128), f32),
            pltpu.VMEM((6, 5, 8, 128), f32),
            pltpu.VMEM((5, 4, 8, 128), f32),
            pltpu.VMEM((16, 24, 128), f32),
            pltpu.VMEM((16, 24, 128), f32),
            pltpu.VMEM((16, 16, 128), f32),
            pltpu.VMEM((16, 16, 128), f32),
            pltpu.VMEM((16, 32, 128), f32),
            pltpu.VMEM((7, 32, 128), f32),
            pltpu.VMEM((8, 32, 128), f32),
            pltpu.VMEM((32, 1, 128), f32),
            pltpu.VMEM((31, 1, 128), f32),
            pltpu.VMEM((128, 1024), jnp.bfloat16),
            pltpu.VMEM((128, 1024), jnp.bfloat16),
            dma((4,)),
            dma((8,)),
            dma((9,)),
            dma((9,)),
            dma((4,)),
            dma((4,)),
        ],
        compiler_params=pltpu.CompilerParams(
            collective_id=0, has_side_effects=True, vmem_limit_bytes=24 << 20
        ),
        name="step",
    )(
        panel_counts,
        in_hbm(panel_cells.reshape(1, panel_cells.shape[0])),
        in_hbm(conserved),
        in_hbm(time_bins.T),
        in_hbm(amplitudes.T),
        in_hbm(jnp.asarray(filter_rows())),
    )
    section, signal = pl.pallas_call(
        leave_kernel,
        out_shape=(
            jax.ShapeDtypeStruct(conserved.shape, f32),
            jax.ShapeDtypeStruct((2, 64), f32),
        ),
        in_specs=[hbm, hbm],
        out_specs=(hbm, hbm),
        scratch_shapes=[dma((6,))],
        compiler_params=pltpu.CompilerParams(vmem_limit_bytes=8 << 20),
        name="leave",
    )(in_vmem(section), in_vmem(signal))
    return (section, signal.T)


def solution(mesh):
    placed = (
        P(None, "ax", "az", None),
        P(("ax", "az")),
        P(("ax", "az")),
        P(("ax", "az"), None),
        P(("ax", "az"), None),
    )
    return jax.shard_map(
        on_device,
        mesh=mesh,
        in_specs=placed,
        out_specs=(P(None, "ax", "az", None), P(None, ("ax", "az"))),
        check_vma=False,
    )
```
